32 devices in a mesh: aux: 8 (over z, x), occ: 4 (over y, core).
Axes of the slice: x: 2, y: 2, z: 4, core: 2. Of those that a mesh axis runs over, the one named last changes fastest.
Arguments:
- blocks: float32 [384, 8, 4096], P('aux', 'occ'), may hold values from -6 to 6
- pair_list: int32 [8, 8, 2], P('aux', 'occ'), may hold values from 0 to 15
- pair_count: int32 [8], P('aux'), may hold values from 2 to 8, as said below
- orbitals: float32 [128, 1024], replicated, may hold values from -0.001953125 to 0.001953125
Outputs:
- exchange: float32 [1024, 1024], P('aux', 'occ')
The draws below stay inside these ranges and needn't reach their ends.
Inputs may be any that keep to these rules, and one draw needn't show every extreme that they name: `pair_list`: block indices of the kept pairs; pairs may repeat. `pair_count`: slots at or beyond an auxiliary block's count are padding and contribute nothing; some auxiliary block uses all 8 slots.
All inputs are finite; a program needn't handle non-finite values.
Results may differ from the reference program's by a relative error of at most 0.0003.
Values sent between devices are 32-bit elements; how exact they have to be, the bound alone decides.
A program may use at most 64 MiB of HBM per device.

```python
import jax
import jax.numpy as jnp
from jax import lax

NBF = 1024
BLK = 64
NOCC = 128
AUX_DEV = 48
NB = 16
KEPT = 8
NAUX = 384
N_AUX = 8


def draw_pair_count(key, part):
    counts = jax.random.randint(key, (N_AUX,), KEPT // 4, KEPT + 1).astype(jnp.int32)
    position = jax.random.randint(jax.random.fold_in(key, 7), (), 0, N_AUX)
    return counts.at[position].set(KEPT).astype(jnp.int32)


def place_ends(drawn, own_key, smallest, high):
    longest = drawn.shape.index(max(drawn.shape))
    spots = []
    for shift in (0, 1):
        where = [jax.random.randint(jax.random.fold_in(own_key, axis), (), 0, length) for axis, length in enumerate(drawn.shape)]
        where[longest] = (where[longest] + shift) % drawn.shape[longest]
        spots.append(tuple(where))
    return drawn.at[spots[0]].set(smallest).at[spots[1]].set(high)


def block_scale(key, shape, pieces, least, high):
    loudness, own = 1.0, jax.random.fold_in(key, 6)
    for dim, blocks in pieces:
        steps = jnp.exp(jax.random.uniform(jax.random.fold_in(own, dim), (blocks,), jnp.float32, least / len(pieces), high / len(pieces)))
        loudness = loudness * jnp.repeat(steps, shape[dim] // blocks).reshape([-1 if axis == dim else 1 for axis in range(len(shape))])
    return loudness


def scatter_about(key, dims, deviation, limit, pieces=(), kind=jnp.bfloat16):
    entries = deviation * jax.random.normal(key, dims, jnp.float32)
    if pieces:
        entries = entries * block_scale(key, dims, pieces, -0.22, 0.18)
    return jnp.clip(entries, -limit, limit).astype(kind)


def setup_inputs(seed: int = 0) -> dict:
    key_of = jax.random.split(jax.random.key(seed), 5)
    blocks = scatter_about(key_of[0], (NAUX, KEPT, BLK * BLK), 1.0, 6.0, ((0, 8), (1, 4)), jnp.float32)
    pair_list = place_ends(jax.random.randint(key_of[1], (N_AUX, KEPT, 2), 0, NB), jax.random.fold_in(key_of[1], 1), 0, NB - 1).astype(jnp.int32)
    pair_count = draw_pair_count(jax.random.fold_in(key_of[4], 71), 0)
    orbitals = scatter_about(key_of[3], (NOCC, NBF), (160 * AUX_DEV * N_AUX * NOCC) ** -0.5, 0.001953125, (), jnp.float32)
    return {"blocks": blocks, "pair_list": pair_list, "pair_count": pair_count, "orbitals": orbitals}


def reference(blocks, pair_list, pair_count, orbitals):
    n_blocks = NBF // BLK
    coefficients = orbitals.reshape(NOCC, n_blocks, BLK)
    tile_data = blocks.reshape(N_AUX, AUX_DEV, KEPT, BLK, BLK)
    positions = jnp.arange(n_blocks, dtype=jnp.int32)
    slot_index = jnp.arange(KEPT, dtype=jnp.int32)

    def one_block(total, inputs):
        tiles_here, pairs_here, count_here = inputs
        live_slot = slot_index < count_here
        row_onehot = ((pairs_here[:, 0][:, None] == positions[None, :]) & live_slot[:, None]).astype(jnp.float32)
        col_onehot = (pairs_here[:, 1][:, None] == positions[None, :]).astype(jnp.float32)
        picked_cols = jnp.einsum('iNn,sN->sin', coefficients, col_onehot, precision=lax.Precision.HIGHEST)
        half_tiles = jnp.einsum('qsmn,sin->isqm', tiles_here, picked_cols, precision=lax.Precision.HIGHEST)
        transformed = jnp.einsum('isqm,sM->iqMm', half_tiles, row_onehot, precision=lax.Precision.HIGHEST)
        transformed = transformed.reshape(NOCC * AUX_DEV, NBF)
        partial_value = jnp.einsum('rm,rn->mn', transformed, transformed, precision=lax.Precision.HIGHEST)
        return total + partial_value, None

    total, _ = lax.scan(one_block, jnp.zeros((NBF, NBF), jnp.float32), (tile_data, pair_list, pair_count))
    return total
```

```python
import functools
import math

import jax
import jax.numpy as jnp
from jax import lax
from jax.experimental import pallas as pl
from jax.experimental.pallas import tpu as pltpu
from jax.sharding import PartitionSpec as P

LANES = 128
PIECES = 2
MESH = pl.DeviceIdType.MESH
NT = (((1,), (1,)), ((), ()))
NN = (((1,), (0,)), ((), ()))


def dot(a, b, dims):
    return lax.dot_general(a, b, dims, preferred_element_type=jnp.float32)


def split(x):
    hi = x.astype(jnp.bfloat16)
    return hi, (x - hi.astype(jnp.float32)).astype(jnp.bfloat16)


def kernel(n_aux, n_occ, n_sub, tiles, pairs_hbm, count_in, orb_hbm, out, pairs_in, orb, rx, rxd, ids, whi, wlo, hhi, hlo,
           dhi, dlo, diag, dcore, dfull, off, ocore, opair, oin, ofull, dense, z_in,
           in_s, local_s, tile_s, tile_r, quart_s, quart_r, ids_s, ids_r, idx_s, idx_r, dc_s, dc_r,
           dx_s, dx_r, dy_s, dy_r, df_s, df_r, dd_s, dd_r, oc_s, oc_r, oy_s, oy_r, ox_s, ox_r,
           op_s, op_r, of_s, of_r, z_s, z_r):
    a, o = lax.axis_index("aux"), lax.axis_index("occ")
    n_y, n_hi = n_occ // 2, n_aux // 2
    y, c = o // 2, lax.rem(o, 2)
    hi_a, lo = a // 2, lax.rem(a, 2)
    own_q = tiles.shape[0] // n_occ
    sub_q = own_q // n_sub
    krows = tiles.shape[1] // 2
    blk = 2 * krows
    side = 4 * blk
    n_slots = 2 * n_occ
    n_off = n_y * (n_y - 1) // 2
    d_half, o_half = side // 2, n_off * side // 2
    piece = o_half // PIECES
    nbf, n_orb = orb.shape[1], orb.shape[0]

    def y_peer(d):
        return lax.rem(y + d, n_y)

    peers = [(d, e) for d in range(1, n_y) for e in (0, 1)] + [(0, 1)]

    def occ_peer(d, e):
        return y_peer(d) * 2 + (c if e == 0 else 1 - c)

    partner = (a, occ_peer(0, 1))
    x_peer = (a + 1 - 2 * lo, o)

    def z_peer(d):
        return (lax.rem(hi_a + d, n_hi) * 2 + lo, o)

    barrier = pltpu.get_barrier_semaphore()
    greet = [(a, occ_peer(*d)) for d in peers] + [x_peer] + [z_peer(d) for d in range(1, n_hi)]
    for dev in greet:
        pl.semaphore_signal(barrier, inc=1, device_id=dev, device_id_type=MESH)

    def local(src, dst, s):
        cp = pltpu.make_async_copy(src, dst, s)
        cp.start()
        return cp

    def quarter(index):
        return tiles.at[pl.ds(index * own_q, own_q)]

    inputs = [local(src, dst, in_s.at[n]) for n, (src, dst) in enumerate(
        ((pairs_hbm, pairs_in), (orb_hbm, orb)))]
    locals_ = [local(quarter(o), rx.at[o], local_s.at[0])]
    for d in range(1, n_y):
        locals_.append(local(quarter(y_peer(d) * 2 + c), rxd.at[c, d - 1], local_s.at[d]))
    pl.semaphore_wait(barrier, len(greet))

    def remote(src, dst, s, r, dev):
        cp = pltpu.make_async_remote_copy(
            src_ref=src, dst_ref=dst, send_sem=s, recv_sem=r, device_id=dev, device_id_type=MESH
        )
        cp.start()
        return cp

    def sub_tiles(j, d, e):
        peer = occ_peer(d, e)
        n = d * 2 + e
        return remote(tiles.at[pl.ds(peer * own_q + j * sub_q, sub_q)], rx.at[o, pl.ds(j * sub_q, sub_q)],
                      tile_s.at[j, n], tile_r.at[j, n], (a, peer))

    def tiles_of(j):
        return [sub_tiles(j, d, e) for d in range(1, n_y) for e in (0, 1)]

    tile_copies = [tiles_of(0)]
    quarters = []
    inputs[0].wait()
    lane1 = lax.broadcasted_iota(jnp.int32, (8, LANES), 1)
    row1 = lax.broadcasted_iota(jnp.int32, (8, LANES), 0)
    within = lax.rem(lane1, blk)
    place = lax.rem(within, krows) * 2 + within // krows
    live = [jnp.where(o * 2 + s < count_in[0], pairs_in[0, s, 0] * blk, -nbf - blk) for s in range(2)]
    cols = jnp.where(row1 == 0, pairs_in[0, 0, 1], pairs_in[0, 1, 1]) * blk + within
    ids[lo, o] = jnp.where(row1 < 2, cols, jnp.where(lane1 < blk, live[0], live[1]) + place)
    id_copies = []
    for n, d in enumerate(peers):
        id_copies.append(remote(ids.at[lo, o], ids.at[lo, o], ids_s.at[n], ids_r.at[n], (a, occ_peer(*d))))
    for d in range(1, n_y):
        quarters.append(remote(quarter(y_peer(d) * 2 + 1 - c), rxd.at[c, d - 1],
                               quart_s.at[d], quart_r.at[d], partner))
    quarters.append(remote(quarter(o + 1 - 2 * c), rx.at[o], quart_s.at[0], quart_r.at[0], partner))
    for j in range(1, n_sub):
        tile_copies.append(tiles_of(j))
    inputs[1].wait()
    orb_hi, orb_lo = split(orb[...])
    row_pos = lax.broadcasted_iota(jnp.int32, (nbf, LANES), 0)
    lane = lax.broadcasted_iota(jnp.int32, (n_orb, LANES), 1)
    def weights(src):
        for s in range(2):
            sel = (row_pos == ids[lo, src, pl.ds(s, 1), :]).astype(jnp.float32).astype(jnp.bfloat16)
            for orb_part, copies, dst in ((orb_hi, 2, whi), (orb_lo, 1, wlo)):
                w = dot(orb_part, sel, NN)
                for p in range(2):
                    keep = lane < blk if p == 0 else lane >= blk
                    w_p = jnp.where(keep, w, 0.0).astype(jnp.bfloat16)
                    for n in range(copies):
                        dst[src * 2 + s, p * n_orb:(p + 1) * n_orb, n * LANES:(n + 1) * LANES] = w_p

    id_copies[-1].wait()
    for e in range(2):
        weights(y * 2 + e)

    def half(load, slot, row0, q0, hi_ref, lo_ref):
        rows = jnp.concatenate([load(q) for q in range(sub_q)], axis=0)
        bh, bl = split(rows)
        wh, wl = whi[slot], wlo[slot]
        res = dot(jnp.concatenate([bh, bl], axis=1), wh, NT) + dot(bh, wl, NT)
        for q in range(sub_q):
            for p in range(2):
                ph, pl_ = split(res[q * krows:(q + 1) * krows, p * n_orb:(p + 1) * n_orb])
                at = pl.ds(pl.multiple_of(row0 + p * krows, krows), krows)
                lanes = slice((q0 + q) * n_orb, (q0 + q + 1) * n_orb)
                hi_ref[at, lanes] = ph
                lo_ref[at, lanes] = pl_

    def gram(hi_i, lo_i, hi_k, lo_k):
        return dot(hi_i, hi_k, NT) + dot(hi_i, lo_k, NT) + dot(lo_i, hi_k, NT)

    for cp in locals_ + quarters:
        cp.wait()
    total = None
    for d in range(1, n_y):
        for j in range(n_sub):
            for e in range(2):
                for s in range(2):
                    half(lambda q: rxd[e, d - 1, j * sub_q + q, pl.ds(s, krows, stride=2), :],
                         (y * 2 + e) * 2 + s, (e * 2 + s) * blk, 0, dhi, dlo)
            val = gram(dhi[...], dlo[...], dhi[...], dlo[...])
            total = val if total is None else total + val
    mine = pl.ds(pl.multiple_of(y * side, side), side)
    for j in range(n_sub):
        for e in range(2):
            for s in range(2):
                half(lambda q: rx[y * 2 + e, j * sub_q + q, pl.ds(s, krows, stride=2), :],
                     (y * 2 + e) * 2 + s, ((y * 2 + e) * 2 + s) * blk, j * sub_q, hhi, hlo)
    total = total + gram(hhi[mine, :], hlo[mine, :], hhi[mine, :], hlo[mine, :])
    diag[...] = total
    cp = remote(diag.at[pl.ds((1 - c) * d_half, d_half)], dcore, dc_s, dc_r, partner)
    cp.wait()
    my_d = pl.ds(pl.multiple_of(c * d_half, d_half), d_half)
    dfull[lo, y, my_d, :] = diag[my_d, :] + dcore[...]
    my_diag = dfull.at[lo, y, my_d]
    dx = [remote(my_diag, my_diag, dx_s, dx_r, x_peer)]
    dys = [remote(my_diag, my_diag, dy_s.at[d], dy_r.at[d], (a, y_peer(d) * 2 + c)) for d in range(1, n_y)]

    for cp in id_copies[:-1]:
        cp.wait()
    idx_copy = remote(ids.at[lo], ids.at[lo], idx_s, idx_r, x_peer)
    for d in range(1, n_y):
        for e in range(2):
            weights(y_peer(d) * 2 + e)
    offs = [(i, k) for i in range(n_y) for k in range(i)]
    for j in range(n_sub):
        for cp in tile_copies[j]:
            cp.wait()
        for d in range(1, n_y):
            for e in range(2):
                for s in range(2):
                    src = y_peer(d) * 2 + e
                    half(lambda q: rx[src, j * sub_q + q, pl.ds(s, krows, stride=2), :],
                         src * 2 + s, (src * 2 + s) * blk, j * sub_q, hhi, hlo)
        at = slice(j * sub_q * n_orb, (j + 1) * sub_q * n_orb)
        for b, (i, k) in enumerate(offs):
            ri, rk = slice(i * side, (i + 1) * side), slice(k * side, (k + 1) * side)
            val = gram(hhi[ri, at], hlo[ri, at], hhi[rk, at], hlo[rk, at])
            if j:
                val = val + off[b * side:(b + 1) * side, :]
            off[b * side:(b + 1) * side, :] = val
    cp = remote(off.at[pl.ds((1 - c) * o_half, o_half)], ocore, oc_s, oc_r, partner)
    cp.wait()
    opair[...] = off[pl.ds(pl.multiple_of(c * o_half, piece), o_half), :] + ocore[...]
    oys = []
    for p in range(PIECES):
        at = pl.ds(p * piece, piece)
        oys.append([remote(opair.at[at], oin.at[d - 1, at], oy_s.at[p, d - 1], oy_r.at[p, d - 1],
                           (a, y_peer(d) * 2 + c)) for d in range(1, n_y)])
    dfs = []
    for d in range(1, n_y):
        dys[d - 1].wait_recv()
        got = dfull.at[lo, y_peer(n_y - d), my_d]
        dfs.append(remote(got, got, df_s.at[d], df_r.at[d], x_peer))
    oxs, ops = [], []
    for p in range(PIECES):
        val = opair[p * piece:(p + 1) * piece, :]
        for d in range(1, n_y):
            oys[p][d - 1].wait()
            val = val + oin[d - 1, p * piece:(p + 1) * piece, :]
        at = pl.ds(pl.multiple_of(c * o_half + p * piece, piece), piece)
        ofull[lo, at, :] = val
        ref = ofull.at[lo, at]
        oxs.append(remote(ref, ref, ox_s.at[p], ox_r.at[p], x_peer))
        ops.append(remote(ref, ref, op_s.at[p], op_r.at[p], partner))
    for cp in dx + dfs:
        cp.wait()
    for cp in dys:
        cp.wait_send()
    idx_copy.wait()
    half_d = dfull.at[:, :, my_d]
    cp = remote(half_d, half_d, dd_s, dd_r, partner)

    out_rows, out_cols = out.shape[1:]
    compact = n_slots * blk
    col_pos = lax.broadcasted_iota(jnp.int32, (out_cols, compact), 0) + o * out_cols
    row_i = lax.broadcasted_iota(jnp.int32, (n_hi * out_rows, compact), 0)
    row_h = lax.rem(row_i // out_rows + 1 + hi_a, n_hi)
    row_pos = (row_h * 2 + lo) * out_rows + lax.rem(row_i, out_rows)
    picks = []
    for l in range(2):
        where = jnp.concatenate([ids[l, s, 2:3, :] for s in range(n_occ)], axis=1)
        picks.append([(pos == where).astype(jnp.float32).astype(jnp.bfloat16) for pos in (col_pos, row_pos)])

    def spread(acc, l, i, t):
        for e in split(t):
            v = dot(picks[l][1][:, i * side:(i + 1) * side], e, NN)
            acc = v if acc is None else acc + v
        return acc

    cp.wait()
    acc = None
    for l in range(2):
        for i in range(n_y):
            dh, dl = split(dfull[l, i])
            cols = picks[l][0][:, i * side:(i + 1) * side]
            acc = spread(acc, l, i, dot(dh, cols, NT) + dot(dl, cols, NT))
    fwd = []
    for p in range(PIECES):
        oxs[p].wait()
        ref = ofull.at[1 - lo, pl.ds(pl.multiple_of(c * o_half + p * piece, piece), piece)]
        fwd.append(remote(ref, ref, of_s.at[p], of_r.at[p], partner))
    for cp in ops + fwd:
        cp.wait()
    parts = []
    for l in range(2):
        t = [None] * n_y
        for b, (i, k) in enumerate(offs):
            for e in split(ofull[l, b * side:(b + 1) * side, :]):
                vi = dot(e, picks[l][0][:, k * side:(k + 1) * side], NT)
                vk = dot(e, picks[l][0][:, i * side:(i + 1) * side], (((0,), (1,)), ((), ())))
                t[i] = vi if t[i] is None else t[i] + vi
                t[k] = vk if t[k] is None else t[k] + vk
        parts.append([split(v) for v in t])
    zs = []
    for g in range(n_hi // 2):
        rows = slice(2 * g * out_rows, 2 * (g + 1) * out_rows)
        v = acc[rows, :]
        for l in range(2):
            for i in range(n_y):
                for e in parts[l][i]:
                    v = v + dot(picks[l][1][rows, i * side:(i + 1) * side], e, NN)
        for n in range(2):
            d = 2 * g + n + 1
            if d < n_hi:
                dense[d - 1] = v[n * out_rows:(n + 1) * out_rows, :]
                zs.append(remote(dense.at[d - 1], z_in.at[d - 1], z_s.at[d - 1], z_r.at[d - 1], z_peer(d)))
            else:
                out[0] = v[n * out_rows:(n + 1) * out_rows, :]
    result = None
    for d in range(1, n_hi):
        zs[d - 1].wait()
        result = z_in[d - 1] if result is None else result + z_in[d - 1]
    out[1] = result


STREAM = 4


def stream_kernel(n_hi, tiles, pairs_hbm, count_in, orb_hbm, out, pairs_in, orb, own, par, rx, ids, w_all, lhi, llo,
                  far, diag, off, p_l, p_f, acc, acc_in, in_s, own_s, par_s, par_r, y_s, y_r, ids_s, ids_r,
                  idz_s, idz_r, dz_s, dz_r, cz_s, cz_r, dd_s, dd_r, oz_s, oz_r, od_s, od_r, xy_s, xy_r):
    a, o = lax.axis_index("aux"), lax.axis_index("occ")
    hi, lo, y, c = a // 2, lax.rem(a, 2), o // 2, lax.rem(o, 2)
    n_q, krows = tiles.shape[0], tiles.shape[1] // 2
    far_q, width = n_q // 2, krows // STREAM
    blk, pair = 2 * krows, 4 * krows
    part = 4 * width
    n_orb, nbf = orb.shape
    out_rows, out_cols = out.shape[1:]
    partner = (a, y * 2 + 1 - c)
    across = (a, (1 - y) * 2 + c)
    mates = [partner, across, (a, (1 - y) * 2 + 1 - c)]
    others = [(hi * 2 + 1 - lo, (1 - y) * 2 + c), (hi * 2 + 1 - lo, o), across]

    def z_peer(d):
        return (lax.rem(hi + d, n_hi) * 2 + lo, o)

    barrier = pltpu.get_barrier_semaphore()
    greet = mates + others[:2] + [z_peer(d) for d in range(1, n_hi)]
    for dev in greet:
        pl.semaphore_signal(barrier, inc=1, device_id=dev, device_id_type=MESH)

    def local(src, dst, s):
        cp = pltpu.make_async_copy(src, dst, s)
        cp.start()
        return cp

    def remote(src, dst, s, r, dev):
        cp = pltpu.make_async_remote_copy(
            src_ref=src, dst_ref=dst, send_sem=s, recv_sem=r, device_id=dev, device_id_type=MESH
        )
        cp.start()
        return cp

    inputs = [local(src, dst, in_s.at[n]) for n, (src, dst) in enumerate(
        ((pairs_hbm, pairs_in), (orb_hbm, orb)))]
    halves = [pl.ds(n * far_q, far_q) for n in range(2)]
    own_copies = [local(tiles.at[h], own.at[h], own_s.at[n]) for n, h in enumerate(halves)]

    inputs[0].wait()
    lane1 = lax.broadcasted_iota(jnp.int32, (8, LANES), 1)
    row1 = lax.broadcasted_iota(jnp.int32, (8, LANES), 0)
    within = lax.rem(lane1, blk)
    place = lax.rem(within, krows) * 2 + within // krows
    live = [jnp.where(o * 2 + s < count_in[0], pairs_in[0, s, 0] * blk, -nbf - blk) for s in range(2)]
    cols = jnp.where(row1 == 0, pairs_in[0, 0, 1], pairs_in[0, 1, 1]) * blk + within
    near = jnp.where(lane1 < blk, live[0], live[1]) + place
    in_part = lax.rem(lane1, part)
    far_place = (lane1 // part * width + lax.rem(lane1, width)) * 2 + lax.rem(in_part, 2 * width) // width
    far_id = jnp.where(in_part < 2 * width, live[0], live[1]) + far_place
    ids[hi, o] = jnp.where(row1 < 2, cols, jnp.where(row1 == 2, near, far_id))

    pl.semaphore_wait(barrier, len(greet))
    mine = ids.at[hi, o]
    id_copies = [remote(mine, mine, ids_s.at[n], ids_r.at[n], dev) for n, dev in enumerate(mates)]
    par_copies = [remote(tiles.at[h], par.at[h], par_s.at[n], par_r.at[n], partner) for n, h in enumerate(halves)]
    far_rows = pl.ds(pl.multiple_of((1 - y) * far_q, far_q), far_q)
    y_copies = [remote(tiles.at[far_rows, pl.ds(j * 2 * width, 2 * width)], rx.at[j], y_s.at[j], y_r.at[j], across)
                for j in range(STREAM)]

    inputs[1].wait()
    orb_hi, orb_lo = split(orb[...])
    row_pos = lax.broadcasted_iota(jnp.int32, (nbf, LANES), 0)
    lane = lax.broadcasted_iota(jnp.int32, (n_orb, LANES), 1)

    def weights(src, base):
        for s in range(2):
            sel = (row_pos == ids[hi, src, pl.ds(s, 1), :]).astype(jnp.float32).astype(jnp.bfloat16)
            for orb_part, spots in ((orb_hi, (0, 1)), (orb_lo, (2,))):
                w = dot(orb_part, sel, NN)
                for p in range(2):
                    keep = lane < blk if p == 0 else lane >= blk
                    w_p = jnp.where(keep, w, 0.0).astype(jnp.bfloat16)
                    for n in spots:
                        w_all[base + s, p * n_orb:(p + 1) * n_orb, n * LANES:(n + 1) * LANES] = w_p

    def transform(rows, slot):
        bh, bl = split(rows)
        return dot(jnp.concatenate([bh, bl, bh], axis=1), w_all[slot], NT)

    batch = math.gcd(far_q, 8)

    def near_half(src, e, base):
        def step(b, carry):
            for s in range(2):
                res = transform(jnp.concatenate(
                    [src[b * batch + q, pl.ds(s, krows, stride=2), :] for q in range(batch)], axis=0), base + s)
                for q in range(batch):
                    lanes = pl.ds(pl.multiple_of((b * batch + q) * n_orb, n_orb), n_orb)
                    for p in range(2):
                        h, l = split(res[q * krows:(q + 1) * krows, p * n_orb:(p + 1) * n_orb])
                        at = pl.ds(pl.multiple_of(e * pair + s * blk + p * krows, krows), krows)
                        lhi[at, lanes] = h
                        llo[at, lanes] = l
            return carry
        return step

    def stacked(both, hi_k):
        v = dot(both, hi_k, NT)
        n = v.shape[0] // 2
        return v[:n], v[n:]

    n_half = far_q // batch
    weights(o, 0)
    for n in range(2):
        own_copies[n].wait()
        lax.fori_loop(n * n_half, (n + 1) * n_half, near_half(own, c, 0), 0)
    at = pl.ds(pl.multiple_of(c * pair, pair), pair)
    v, u = stacked(jnp.concatenate([lhi[at, :], llo[at, :]], axis=0), lhi[at, :])
    diag[hi, c, 0:pair, :] = v + (u + u.T)
    ref = diag.at[hi, c, pl.ds(0, pair)]
    dz = [remote(ref, ref, dz_s.at[d - 1], dz_r.at[d - 1], z_peer(d)) for d in range(1, n_hi)]

    id_copies[0].wait()
    weights(y * 2 + 1 - c, 2)
    for n in range(2):
        par_copies[n].wait()
        lax.fori_loop(n * n_half, (n + 1) * n_half, near_half(par, 1 - c, 2), 0)
    at = pl.ds(pl.multiple_of(c * blk, blk), blk)
    right = slice(pair, 2 * pair)
    v, u = stacked(jnp.concatenate([lhi[at, :], llo[at, :]], axis=0), lhi[right, :])
    diag[hi, c, pair:pair + blk, :] = v + u + dot(lhi[at, :], llo[right, :], NT)
    ref = diag.at[hi, c, pl.ds(pair, blk)]
    dz += [remote(ref, ref, cz_s.at[d - 1], cz_r.at[d - 1], z_peer(d)) for d in range(1, n_hi)]

    for cp in id_copies[1:]:
        cp.wait()
    ref = ids.at[hi]
    idz = [remote(ref, ref, idz_s.at[d - 1], idz_r.at[d - 1], z_peer(d)) for d in range(1, n_hi)]
    weights((1 - y) * 2 + c, 4)
    near_q = pl.ds(pl.multiple_of(y * far_q * n_orb, LANES), far_q * n_orb)

    def stream(j):
        y_copies[j].wait()
        for s in range(2):
            res = transform(jnp.concatenate(
                [rx[j, q, pl.ds(s, width, stride=2), :] for q in range(far_q)], axis=0), 4 + s)
            for q in range(far_q):
                rows = res[q * width:(q + 1) * width, :]
                h, l = split(jnp.concatenate([rows[:, :n_orb], rows[:, n_orb:]], axis=0))
                far[s * 2 * width:(s + 1) * 2 * width, q * n_orb:(q + 1) * n_orb] = h
                far[part + s * 2 * width:part + (s + 1) * 2 * width, q * n_orb:(q + 1) * n_orb] = l
        v, u = stacked(far[...], lhi[:, near_q])
        off[hi, c, j] = v + u + dot(far[0:part, :], llo[:, near_q], NT)
        ref = off.at[hi, c, j]
        return [remote(ref, ref, oz_s.at[j, d - 1], oz_r.at[j, d - 1], z_peer(d)) for d in range(1, n_hi)]

    def share(copies, ref, s, r):
        for cp in copies:
            cp.wait()
        return remote(ref, ref, s, r, partner)

    def share_off(j):
        return share(oz[j], off.at[:, c, j], od_s.at[j], od_r.at[j])

    def onehot(pos, where):
        return (pos == where).astype(jnp.float32).astype(jnp.bfloat16)

    n_row = 2 * out_rows

    def positions(n):
        r = lax.broadcasted_iota(jnp.int32, (n_row, n), 0) + hi * n_row
        col = lax.broadcasted_iota(jnp.int32, (out_cols, n), 0)
        return [r] + [col + (h * 2 + c) * out_cols for h in range(2)]

    def place_ids():
        spans = [slice(0, n_row)] + [slice(n_row + h * out_cols, n_row + (h + 1) * out_cols) for h in range(2)]
        pos = positions(2 * pair)
        for g in range(n_hi):
            where = jnp.concatenate([ids[g, y * 2 + e, 2:3, :] for e in range(2)], axis=1)
            for span, at in zip(spans, pos):
                p_l[g, span, :] = onehot(at, where)
        pos = positions(n_hi * 2 * part)
        for j in range(STREAM):
            where = jnp.concatenate([ids[g, (1 - y) * 2 + e, 3:4, j * part:(j + 1) * part]
                                     for g in range(n_hi) for e in range(2)], axis=1)
            for span, at in zip(spans, pos):
                p_f[j, span, :] = onehot(at, where)

    def expand_diag():
        total = [None, None]
        for g in range(n_hi):
            rows = [p_l[g, 0:n_row, e * pair:(e + 1) * pair] for e in range(2)]
            cross = jnp.concatenate([diag[g, e, pair:pair + blk, :] for e in range(2)], axis=0)
            t = [None, None]
            for e in range(2):
                for v in split(diag[g, e, 0:pair, :]):
                    v = dot(rows[e], v, NN)
                    t[e] = v if t[e] is None else t[e] + v
            for v in split(cross):
                t[1] = t[1] + dot(rows[0], v, NN)
                t[0] = t[0] + dot(rows[1], v, NT)
            for v in split(jnp.concatenate(t, axis=1)):
                for h in range(2):
                    u = dot(v, p_l[g, n_row + h * out_cols:n_row + (h + 1) * out_cols, :], NT)
                    total[h] = u if total[h] is None else total[h] + u
        for h in range(2):
            for x in range(2):
                acc[x, h] = total[h][x * out_rows:(x + 1) * out_rows, :]

    def spread(j):
        rows, cols = [], [[], []]
        for g in range(n_hi):
            v = jnp.concatenate(split(jnp.concatenate([off[g, e, j] for e in range(2)], axis=0)), axis=0)
            v = dot(v, p_l[g], NT)
            v = v[:2 * part] + v[2 * part:]
            rows.append(v[:, 0:n_row])
            for h in range(2):
                cols[h].append(v[:, n_row + h * out_cols:n_row + (h + 1) * out_cols])
        return (split(jnp.concatenate(rows, axis=0)),
                [split(jnp.concatenate(v, axis=0)) for v in cols])

    tn = (((0,), (1,)), ((), ()))

    def expand_off(j):
        rows, cols = spread(j)
        for h in range(2):
            pick = p_f[j, n_row + h * out_cols:n_row + (h + 1) * out_cols, :]
            v = dot(p_f[j, 0:n_row, :], cols[h][0], NN) + dot(p_f[j, 0:n_row, :], cols[h][1], NN)
            v = v + dot(rows[0], pick, tn) + dot(rows[1], pick, tn)
            for x in range(2):
                acc[x, h] += v[x * out_rows:(x + 1) * out_rows, :]

    oz, od = [], []
    oz.append(stream(0))
    dd = share(dz, diag.at[:, c], dd_s, dd_r)
    for cp in idz:
        cp.wait()
    place_ids()
    oz.append(stream(1))
    od.append(share_off(0))
    dd.wait()
    expand_diag()
    for j in range(2, STREAM):
        oz.append(stream(j))
        od.append(share_off(j - 1))
        od[j - 2].wait()
        expand_off(j - 2)
    od[STREAM - 2].wait()
    expand_off(STREAM - 2)
    od.append(share_off(STREAM - 1))
    od[STREAM - 1].wait()
    expand_off(STREAM - 1)
    sends = []
    for n, (x, h) in enumerate(((1 - lo, 1 - y), (1 - lo, y), (lo, 1 - y))):
        sends.append(remote(acc.at[x, h], acc_in.at[n], xy_s.at[n], xy_r.at[n], others[n]))
    out[0] = acc[lo, y]
    for cp in sends:
        cp.wait()
    out[1] = acc_in[0] + acc_in[1] + acc_in[2]


def stream_call(n_hi, tiles, pair_list, pair_count, orbitals, out_rows, out_cols):
    n_q, rows2, _ = tiles.shape
    n_orb, _ = orbitals.shape
    krows = rows2 // 2
    far_q, width = n_q // 2, krows // STREAM
    blk, pair, part = 2 * krows, 4 * krows, 4 * width
    n_pos = 2 * out_rows + 2 * out_cols
    f32, bf16, dma, vmem = jnp.float32, jnp.bfloat16, pltpu.SemaphoreType.DMA, pltpu.VMEM
    z = n_hi - 1
    sems = [(2,)] * 4 + [(STREAM,)] * 2 + [(3,)] * 2 + [(z,)] * 6 + [()] * 2 + [(STREAM, z)] * 2 + [(STREAM,)] * 2
    sems += [(3,)] * 2
    return pl.pallas_call(
        functools.partial(stream_kernel, n_hi),
        name="exchange",
        out_shape=jax.ShapeDtypeStruct((2, out_rows, out_cols), f32),
        in_specs=[pl.BlockSpec(memory_space=space) for space in (pl.ANY, pl.ANY, pltpu.SMEM, pl.ANY)],
        out_specs=pl.BlockSpec(memory_space=vmem),
        scratch_shapes=[
            pltpu.SMEM(pair_list.shape, jnp.int32),
            vmem(orbitals.shape, f32),
            vmem(tiles.shape, f32),
            vmem(tiles.shape, f32),
            vmem((STREAM, far_q, 2 * width, LANES), f32),
            vmem((n_hi, 4, 8, LANES), jnp.int32),
            vmem((6, 2 * n_orb, 3 * LANES), bf16),
            vmem((2 * pair, n_q * n_orb), bf16),
            vmem((2 * pair, n_q * n_orb), bf16),
            vmem((2 * part, far_q * n_orb), bf16),
            vmem((n_hi, 2, pair + blk, LANES), f32),
            vmem((n_hi, 2, STREAM, part, 2 * pair), f32),
            vmem((n_hi, n_pos, 2 * pair), bf16),
            vmem((STREAM, n_pos, n_hi * 2 * part), bf16),
            vmem((2, 2, out_rows, out_cols), f32),
            vmem((3, out_rows, out_cols), f32),
        ] + [dma(s) for s in sems],
        compiler_params=pltpu.CompilerParams(collective_id=0, has_side_effects=True),
    )(tiles, pair_list, pair_count, orbitals)


def per_device(n_aux, n_occ, blocks, pair_list, pair_count, orbitals):
    n_q, slots, area = blocks.shape
    n_orb, nbf = orbitals.shape
    krows = area // LANES
    blk = 2 * krows
    tiles = blocks.reshape(n_q, slots, krows, LANES).transpose(0, 2, 1, 3).reshape(n_q, krows * slots, LANES)
    if n_occ == 4 and slots * blk == LANES:
        sums = stream_call(n_aux // 2, tiles, pair_list, pair_count, orbitals, nbf // n_aux, nbf // n_occ)
        return sums[0] + sums[1]
    own_q = n_q // n_occ
    n_sub = math.gcd(own_q, 6)
    sub_k = own_q // n_sub * n_orb
    compact = slots * n_occ * blk
    side = 2 * slots * blk
    n_y, n_hi = n_occ // 2, n_aux // 2
    off_rows = n_y * (n_y - 1) // 2 * side
    out_rows, out_cols = nbf // n_aux, nbf // n_occ
    f32, bf16, dma, vmem = jnp.float32, jnp.bfloat16, pltpu.SemaphoreType.DMA, pltpu.VMEM
    sems = [(2,), (n_y,)] + [(n_sub, n_occ)] * 2 + [(n_y,)] * 2 + [(n_occ - 1,)] * 2 + [()] * 6 + [(n_y,)] * 4
    sems += [()] * 4 + [(PIECES, n_y - 1)] * 2 + [(PIECES,)] * 6 + [(n_hi - 1,)] * 2
    sums = pl.pallas_call(
        functools.partial(kernel, n_aux, n_occ, n_sub),
        name="exchange",
        out_shape=jax.ShapeDtypeStruct((2, out_rows, out_cols), f32),
        in_specs=[pl.BlockSpec(memory_space=space) for space in (pl.ANY, pl.ANY, pltpu.SMEM, pl.ANY)],
        out_specs=pl.BlockSpec(memory_space=vmem),
        scratch_shapes=[
            pltpu.SMEM(pair_list.shape, jnp.int32),
            vmem(orbitals.shape, f32),
            vmem((n_occ, own_q, krows * slots, LANES), f32),
            vmem((2, n_y - 1, own_q, krows * slots, LANES), f32),
            vmem((2, n_occ, 8, LANES), jnp.int32),
            vmem((slots * n_occ, 2 * n_orb, 2 * LANES), bf16),
            vmem((slots * n_occ, 2 * n_orb, LANES), bf16),
            vmem((compact, own_q * n_orb), bf16),
            vmem((compact, own_q * n_orb), bf16),
            vmem((side, sub_k), bf16),
            vmem((side, sub_k), bf16),
            vmem((side, side), f32),
            vmem((side // 2, side), f32),
            vmem((2, n_y, side, side), f32),
            vmem((off_rows, side), f32),
            vmem((off_rows // 2, side), f32),
            vmem((off_rows // 2, side), f32),
            vmem((n_y - 1, off_rows // 2, side), f32),
            vmem((2, off_rows, side), f32),
            vmem((n_hi - 1, out_rows, out_cols), f32),
            vmem((n_hi - 1, out_rows, out_cols), f32),
        ] + [dma(s) for s in sems],
        compiler_params=pltpu.CompilerParams(collective_id=0, has_side_effects=True),
    )(tiles, pair_list, pair_count, orbitals)
    return sums[0] + sums[1]


def solution(mesh):
    body = functools.partial(per_device, mesh.shape["aux"], mesh.shape["occ"])
    in_specs = (P("aux", "occ", None), P("aux", "occ", None), P("aux"), P())
    return jax.shard_map(body, mesh=mesh, in_specs=in_specs, out_specs=P("aux", "occ"), check_vma=False)
```

```python
import functools
import math

import jax
import jax.numpy as jnp
from jax import lax
from jax.experimental import pallas as pl
from jax.experimental.pallas import tpu as pltpu
from jax.sharding import PartitionSpec as P

LANES = 128
PIECES = 2
MESH = pl.DeviceIdType.MESH
NT = (((1,), (1,)), ((), ()))
NN = (((1,), (0,)), ((), ()))


def dot(a, b, dims):
    return lax.dot_general(a, b, dims, preferred_element_type=jnp.float32)


def split(x):
    hi = x.astype(jnp.bfloat16)
    return hi, (x - hi.astype(jnp.float32)).astype(jnp.bfloat16)


def kernel(n_aux, n_occ, n_sub, tiles, pairs_hbm, count_in, orb_hbm, out, pairs_in, orb, rx, rxd, ids, whi, wlo, hhi, hlo,
           dhi, dlo, diag, dcore, dfull, off, ocore, opair, oin, ofull, dense, z_in,
           in_s, local_s, tile_s, tile_r, quart_s, quart_r, ids_s, ids_r, idx_s, idx_r, dc_s, dc_r,
           dx_s, dx_r, dy_s, dy_r, df_s, df_r, dd_s, dd_r, oc_s, oc_r, oy_s, oy_r, ox_s, ox_r,
           op_s, op_r, of_s, of_r, z_s, z_r):
    a, o = lax.axis_index("aux"), lax.axis_index("occ")
    n_y, n_hi = n_occ // 2, n_aux // 2
    y, c = o // 2, lax.rem(o, 2)
    hi_a, lo = a // 2, lax.rem(a, 2)
    own_q = tiles.shape[0] // n_occ
    sub_q = own_q // n_sub
    krows = tiles.shape[1] // 2
    blk = 2 * krows
    side = 4 * blk
    n_slots = 2 * n_occ
    n_off = n_y * (n_y - 1) // 2
    d_half, o_half = side // 2, n_off * side // 2
    piece = o_half // PIECES
    nbf, n_orb = orb.shape[1], orb.shape[0]

    def y_peer(d):
        return lax.rem(y + d, n_y)

    peers = [(d, e) for d in range(1, n_y) for e in (0, 1)] + [(0, 1)]

    def occ_peer(d, e):
        return y_peer(d) * 2 + (c if e == 0 else 1 - c)

    partner = (a, occ_peer(0, 1))
    x_peer = (a + 1 - 2 * lo, o)

    def z_peer(d):
        return (lax.rem(hi_a + d, n_hi) * 2 + lo, o)

    barrier = pltpu.get_barrier_semaphore()
    greet = [(a, occ_peer(*d)) for d in peers] + [x_peer] + [z_peer(d) for d in range(1, n_hi)]
    for dev in greet:
        pl.semaphore_signal(barrier, inc=1, device_id=dev, device_id_type=MESH)

    def local(src, dst, s):
        cp = pltpu.make_async_copy(src, dst, s)
        cp.start()
        return cp

    def quarter(index):
        return tiles.at[pl.ds(index * own_q, own_q)]

    inputs = [local(src, dst, in_s.at[n]) for n, (src, dst) in enumerate(
        ((pairs_hbm, pairs_in), (orb_hbm, orb)))]
    locals_ = [local(quarter(o), rx.at[o], local_s.at[0])]
    for d in range(1, n_y):
        locals_.append(local(quarter(y_peer(d) * 2 + c), rxd.at[c, d - 1], local_s.at[d]))
    pl.semaphore_wait(barrier, len(greet))

    def remote(src, dst, s, r, dev):
        cp = pltpu.make_async_remote_copy(
            src_ref=src, dst_ref=dst, send_sem=s, recv_sem=r, device_id=dev, device_id_type=MESH
        )
        cp.start()
        return cp

    def sub_tiles(j, d, e):
        peer = occ_peer(d, e)
        n = d * 2 + e
        return remote(tiles.at[pl.ds(peer * own_q + j * sub_q, sub_q)], rx.at[o, pl.ds(j * sub_q, sub_q)],
                      tile_s.at[j, n], tile_r.at[j, n], (a, peer))

    def tiles_of(j):
        return [sub_tiles(j, d, e) for d in range(1, n_y) for e in (0, 1)]

    tile_copies = [tiles_of(0)]
    quarters = []
    inputs[0].wait()
    lane1 = lax.broadcasted_iota(jnp.int32, (8, LANES), 1)
    row1 = lax.broadcasted_iota(jnp.int32, (8, LANES), 0)
    within = lax.rem(lane1, blk)
    place = lax.rem(within, krows) * 2 + within // krows
    live = [jnp.where(o * 2 + s < count_in[0], pairs_in[0, s, 0] * blk, -nbf - blk) for s in range(2)]
    cols = jnp.where(row1 == 0, pairs_in[0, 0, 1], pairs_in[0, 1, 1]) * blk + within
    ids[lo, o] = jnp.where(row1 < 2, cols, jnp.where(lane1 < blk, live[0], live[1]) + place)
    id_copies = []
    for n, d in enumerate(peers):
        id_copies.append(remote(ids.at[lo, o], ids.at[lo, o], ids_s.at[n], ids_r.at[n], (a, occ_peer(*d))))
    for d in range(1, n_y):
        quarters.append(remote(quarter(y_peer(d) * 2 + 1 - c), rxd.at[c, d - 1],
                               quart_s.at[d], quart_r.at[d], partner))
    quarters.append(remote(quarter(o + 1 - 2 * c), rx.at[o], quart_s.at[0], quart_r.at[0], partner))
    for j in range(1, n_sub):
        tile_copies.append(tiles_of(j))
    inputs[1].wait()
    orb_hi, orb_lo = split(orb[...])
    row_pos = lax.broadcasted_iota(jnp.int32, (nbf, LANES), 0)
    lane = lax.broadcasted_iota(jnp.int32, (n_orb, LANES), 1)
    def weights(src):
        for s in range(2):
            sel = (row_pos == ids[lo, src, pl.ds(s, 1), :]).astype(jnp.float32).astype(jnp.bfloat16)
            for orb_part, copies, dst in ((orb_hi, 2, whi), (orb_lo, 1, wlo)):
                w = dot(orb_part, sel, NN)
                for p in range(2):
                    keep = lane < blk if p == 0 else lane >= blk
                    w_p = jnp.where(keep, w, 0.0).astype(jnp.bfloat16)
                    for n in range(copies):
                        dst[src * 2 + s, p * n_orb:(p + 1) * n_orb, n * LANES:(n + 1) * LANES] = w_p

    id_copies[-1].wait()
    for e in range(2):
        weights(y * 2 + e)

    def half(load, slot, row0, q0, hi_ref, lo_ref):
        rows = jnp.concatenate([load(q) for q in range(sub_q)], axis=0)
        bh, bl = split(rows)
        wh, wl = whi[slot], wlo[slot]
        res = dot(jnp.concatenate([bh, bl], axis=1), wh, NT) + dot(bh, wl, NT)
        for q in range(sub_q):
            for p in range(2):
                ph, pl_ = split(res[q * krows:(q + 1) * krows, p * n_orb:(p + 1) * n_orb])
                at = pl.ds(pl.multiple_of(row0 + p * krows, krows), krows)
                lanes = slice((q0 + q) * n_orb, (q0 + q + 1) * n_orb)
                hi_ref[at, lanes] = ph
                lo_ref[at, lanes] = pl_

    def gram(hi_i, lo_i, hi_k, lo_k):
        return dot(hi_i, hi_k, NT) + dot(hi_i, lo_k, NT) + dot(lo_i, hi_k, NT)

    for cp in locals_ + quarters:
        cp.wait()
    total = None
    for d in range(1, n_y):
        for j in range(n_sub):
            for e in range(2):
                for s in range(2):
                    half(lambda q: rxd[e, d - 1, j * sub_q + q, pl.ds(s, krows, stride=2), :],
                         (y * 2 + e) * 2 + s, (e * 2 + s) * blk, 0, dhi, dlo)
            val = gram(dhi[...], dlo[...], dhi[...], dlo[...])
            total = val if total is None else total + val
    mine = pl.ds(pl.multiple_of(y * side, side), side)
    for j in range(n_sub):
        for e in range(2):
            for s in range(2):
                half(lambda q: rx[y * 2 + e, j * sub_q + q, pl.ds(s, krows, stride=2), :],
                     (y * 2 + e) * 2 + s, ((y * 2 + e) * 2 + s) * blk, j * sub_q, hhi, hlo)
    total = total + gram(hhi[mine, :], hlo[mine, :], hhi[mine, :], hlo[mine, :])
    diag[...] = total
    cp = remote(diag.at[pl.ds((1 - c) * d_half, d_half)], dcore, dc_s, dc_r, partner)
    cp.wait()
    my_d = pl.ds(pl.multiple_of(c * d_half, d_half), d_half)
    dfull[lo, y, my_d, :] = diag[my_d, :] + dcore[...]
    my_diag = dfull.at[lo, y, my_d]
    dx = [remote(my_diag, my_diag, dx_s, dx_r, x_peer)]
    dys = [remote(my_diag, my_diag, dy_s.at[d], dy_r.at[d], (a, y_peer(d) * 2 + c)) for d in range(1, n_y)]

    for cp in id_copies[:-1]:
        cp.wait()
    idx_copy = remote(ids.at[lo], ids.at[lo], idx_s, idx_r, x_peer)
    for d in range(1, n_y):
        for e in range(2):
            weights(y_peer(d) * 2 + e)
    offs = [(i, k) for i in range(n_y) for k in range(i)]
    for j in range(n_sub):
        for cp in tile_copies[j]:
            cp.wait()
        for d in range(1, n_y):
            for e in range(2):
                for s in range(2):
                    src = y_peer(d) * 2 + e
                    half(lambda q: rx[src, j * sub_q + q, pl.ds(s, krows, stride=2), :],
                         src * 2 + s, (src * 2 + s) * blk, j * sub_q, hhi, hlo)
        at = slice(j * sub_q * n_orb, (j + 1) * sub_q * n_orb)
        for b, (i, k) in enumerate(offs):
            ri, rk = slice(i * side, (i + 1) * side), slice(k * side, (k + 1) * side)
            val = gram(hhi[ri, at], hlo[ri, at], hhi[rk, at], hlo[rk, at])
            if j:
                val = val + off[b * side:(b + 1) * side, :]
            off[b * side:(b + 1) * side, :] = val
    cp = remote(off.at[pl.ds((1 - c) * o_half, o_half)], ocore, oc_s, oc_r, partner)
    cp.wait()
    opair[...] = off[pl.ds(pl.multiple_of(c * o_half, piece), o_half), :] + ocore[...]
    oys = []
    for p in range(PIECES):
        at = pl.ds(p * piece, piece)
        oys.append([remote(opair.at[at], oin.at[d - 1, at], oy_s.at[p, d - 1], oy_r.at[p, d - 1],
                           (a, y_peer(d) * 2 + c)) for d in range(1, n_y)])
    dfs = []
    for d in range(1, n_y):
        dys[d - 1].wait_recv()
        got = dfull.at[lo, y_peer(n_y - d), my_d]
        dfs.append(remote(got, got, df_s.at[d], df_r.at[d], x_peer))
    oxs, ops = [], []
    for p in range(PIECES):
        val = opair[p * piece:(p + 1) * piece, :]
        for d in range(1, n_y):
            oys[p][d - 1].wait()
            val = val + oin[d - 1, p * piece:(p + 1) * piece, :]
        at = pl.ds(pl.multiple_of(c * o_half + p * piece, piece), piece)
        ofull[lo, at, :] = val
        ref = ofull.at[lo, at]
        oxs.append(remote(ref, ref, ox_s.at[p], ox_r.at[p], x_peer))
        ops.append(remote(ref, ref, op_s.at[p], op_r.at[p], partner))
    for cp in dx + dfs:
        cp.wait()
    for cp in dys:
        cp.wait_send()
    idx_copy.wait()
    half_d = dfull.at[:, :, my_d]
    cp = remote(half_d, half_d, dd_s, dd_r, partner)

    out_rows, out_cols = out.shape[1:]
    compact = n_slots * blk
    col_pos = lax.broadcasted_iota(jnp.int32, (out_cols, compact), 0) + o * out_cols
    row_i = lax.broadcasted_iota(jnp.int32, (n_hi * out_rows, compact), 0)
    row_h = lax.rem(row_i // out_rows + 1 + hi_a, n_hi)
    row_pos = (row_h * 2 + lo) * out_rows + lax.rem(row_i, out_rows)
    picks = []
    for l in range(2):
        where = jnp.concatenate([ids[l, s, 2:3, :] for s in range(n_occ)], axis=1)
        picks.append([(pos == where).astype(jnp.float32).astype(jnp.bfloat16) for pos in (col_pos, row_pos)])

    def spread(acc, l, i, t):
        for e in split(t):
            v = dot(picks[l][1][:, i * side:(i + 1) * side], e, NN)
            acc = v if acc is None else acc + v
        return acc

    cp.wait()
    acc = None
    for l in range(2):
        for i in range(n_y):
            dh, dl = split(dfull[l, i])
            cols = picks[l][0][:, i * side:(i + 1) * side]
            acc = spread(acc, l, i, dot(dh, cols, NT) + dot(dl, cols, NT))
    fwd = []
    for p in range(PIECES):
        oxs[p].wait()
        ref = ofull.at[1 - lo, pl.ds(pl.multiple_of(c * o_half + p * piece, piece), piece)]
        fwd.append(remote(ref, ref, of_s.at[p], of_r.at[p], partner))
    for cp in ops + fwd:
        cp.wait()
    parts = []
    for l in range(2):
        t = [None] * n_y
        for b, (i, k) in enumerate(offs):
            for e in split(ofull[l, b * side:(b + 1) * side, :]):
                vi = dot(e, picks[l][0][:, k * side:(k + 1) * side], NT)
                vk = dot(e, picks[l][0][:, i * side:(i + 1) * side], (((0,), (1,)), ((), ())))
                t[i] = vi if t[i] is None else t[i] + vi
                t[k] = vk if t[k] is None else t[k] + vk
        parts.append([split(v) for v in t])
    zs = []
    for g in range(n_hi // 2):
        rows = slice(2 * g * out_rows, 2 * (g + 1) * out_rows)
        v = acc[rows, :]
        for l in range(2):
            for i in range(n_y):
                for e in parts[l][i]:
                    v = v + dot(picks[l][1][rows, i * side:(i + 1) * side], e, NN)
        for n in range(2):
            d = 2 * g + n + 1
            if d < n_hi:
                dense[d - 1] = v[n * out_rows:(n + 1) * out_rows, :]
                zs.append(remote(dense.at[d - 1], z_in.at[d - 1], z_s.at[d - 1], z_r.at[d - 1], z_peer(d)))
            else:
                out[0] = v[n * out_rows:(n + 1) * out_rows, :]
    result = None
    for d in range(1, n_hi):
        zs[d - 1].wait()
        result = z_in[d - 1] if result is None else result + z_in[d - 1]
    out[1] = result


SHARES = (3, 2, 2, 1)
STREAM = len(SHARES)


def chunks(krows):
    unit, first = krows // sum(SHARES), 0
    spans = []
    for share in SHARES:
        spans.append((first * unit, share * unit))
        first += share
    return spans


def stream_kernel(n_hi, tiles, pairs_hbm, count_in, orb_hbm, out, pairs_in, orb, own, par, rx, ids, w_all, lhi, llo,
                  far, diag, off, p_l, p_f, acc, acc_in, in_s, own_s, par_s, par_r, y_s, y_r, ids_s, ids_r,
                  idz_s, idz_r, dz_s, dz_r, cz_s, cz_r, dd_s, dd_r, oz_s, oz_r, od_s, od_r, xy_s, xy_r, ready):
    a, o = lax.axis_index("aux"), lax.axis_index("occ")
    hi, lo, y, c = a // 2, lax.rem(a, 2), o // 2, lax.rem(o, 2)
    n_q, krows = tiles.shape[0], tiles.shape[1] // 2
    far_q, spans = n_q // 2, chunks(krows)
    blk, pair = 2 * krows, 4 * krows
    n_orb, nbf = orb.shape
    out_rows, out_cols = out.shape[1:]
    partner = (a, y * 2 + 1 - c)
    across = (a, (1 - y) * 2 + c)
    x_peer = (hi * 2 + 1 - lo, o)
    others = [(hi * 2 + 1 - lo, (1 - y) * 2 + c), x_peer, across]

    def z_peer(d):
        return (lax.rem(hi + d, n_hi) * 2 + lo, o)

    barrier = pltpu.get_barrier_semaphore()
    n_near = jnp.where(hi > 0, 1, 0) + jnp.where(hi < n_hi - 1, 1, 0)

    def greet(sem, devices):
        for dev in devices:
            pl.semaphore_signal(sem, inc=1, device_id=dev, device_id_type=MESH)

        @pl.when(hi > 0)
        def _():
            pl.semaphore_signal(sem, inc=1, device_id=(a - 2, o), device_id_type=MESH)

        @pl.when(hi < n_hi - 1)
        def _():
            pl.semaphore_signal(sem, inc=1, device_id=(a + 2, o), device_id_type=MESH)

    greet(barrier, [partner, across, x_peer])

    def local(src, dst, s):
        cp = pltpu.make_async_copy(src, dst, s)
        cp.start()
        return cp

    def remote(src, dst, s, r, dev):
        cp = pltpu.make_async_remote_copy(
            src_ref=src, dst_ref=dst, send_sem=s, recv_sem=r, device_id=dev, device_id_type=MESH
        )
        cp.start()
        return cp

    inputs = [local(src, dst, in_s.at[n]) for n, (src, dst) in enumerate(
        ((pairs_hbm, pairs_in), (orb_hbm, orb)))]
    halves = [pl.ds(n * far_q, far_q) for n in range(2)]
    own_copies = [local(tiles.at[h], own.at[h], own_s.at[n]) for n, h in enumerate(halves)]

    inputs[0].wait()
    lane1 = lax.broadcasted_iota(jnp.int32, (8, LANES), 1)
    row1 = lax.broadcasted_iota(jnp.int32, (8, LANES), 0)
    within = lax.rem(lane1, blk)
    place = lax.rem(within, krows) * 2 + within // krows
    live = [jnp.where(o * 2 + s < count_in[0], pairs_in[0, s, 0] * blk, -nbf - blk) for s in range(2)]
    cols = jnp.where(row1 == 0, pairs_in[0, 0, 1], pairs_in[0, 1, 1]) * blk + within
    near = jnp.where(lane1 < blk, live[0], live[1]) + place
    far_id = jnp.zeros((8, LANES), jnp.int32)
    for first, width in spans:
        at = lane1 - 4 * first
        tile_row = first * 2 + lax.rem(at, 2 * width)
        spot = jnp.where(lax.rem(tile_row, 2) == 0, live[0], live[1]) + tile_row // 2 * 2 + at // (2 * width)
        far_id = jnp.where((at >= 0) & (at < 4 * width), spot, far_id)
    ids[hi, o] = jnp.where(row1 < 2, cols, jnp.where(row1 == 2, near, far_id))

    pl.semaphore_wait(barrier, 3 + n_near)
    mine = ids.at[hi, o]

    id_copies = [remote(mine, mine, ids_s.at[n], ids_r.at[n], dev) for n, dev in enumerate((partner, across))]
    far_rows = pl.ds(pl.multiple_of((1 - y) * far_q, far_q), far_q)
    y_copies = [remote(tiles.at[far_rows, pl.ds(2 * first, 2 * width)], rx.at[:, pl.ds(2 * first, 2 * width)],
                       y_s.at[j], y_r.at[j], across) for j, (first, width) in enumerate(spans)]
    par_copies = [remote(tiles.at[h], par.at[h], par_s.at[n], par_r.at[n], partner) for n, h in enumerate(halves)]
    greet(ready.at[0], [partner, x_peer])
    inputs[1].wait()
    orb_hi, orb_lo = split(orb[...])
    row_pos = lax.broadcasted_iota(jnp.int32, (nbf, LANES), 0)
    lane = lax.broadcasted_iota(jnp.int32, (n_orb, LANES), 1)

    def weights(src, base):
        for s in range(2):
            sel = (row_pos == ids[hi, src, pl.ds(s, 1), :]).astype(jnp.float32).astype(jnp.bfloat16)
            for orb_part, spots in ((orb_hi, (0, 1)), (orb_lo, (2,))):
                w = dot(orb_part, sel, NN)
                for p in range(2):
                    keep = lane < blk if p == 0 else lane >= blk
                    w_p = jnp.where(keep, w, 0.0).astype(jnp.bfloat16)
                    for n in spots:
                        w_all[base + s, p * n_orb:(p + 1) * n_orb, n * LANES:(n + 1) * LANES] = w_p

    def transform(rows, slot):
        bh, bl = split(rows)
        return dot(jnp.concatenate([bh, bl, bh], axis=1), w_all[slot], NT)

    batch = math.gcd(far_q, 8)

    def near_half(src, e, base):
        def step(b, carry):
            for s in range(2):
                res = transform(jnp.concatenate(
                    [src[b * batch + q, pl.ds(s, krows, stride=2), :] for q in range(batch)], axis=0), base + s)
                for q in range(batch):
                    lanes = pl.ds(pl.multiple_of((b * batch + q) * n_orb, n_orb), n_orb)
                    for p in range(2):
                        h, l = split(res[q * krows:(q + 1) * krows, p * n_orb:(p + 1) * n_orb])
                        at = pl.ds(pl.multiple_of(e * pair + s * blk + p * krows, krows), krows)
                        lhi[at, lanes] = h
                        llo[at, lanes] = l
            return carry
        return step

    def stacked(both, hi_k):
        v = dot(both, hi_k, NT)
        n = v.shape[0] // 2
        return v[:n], v[n:]

    n_half = far_q // batch
    weights(o, 0)

    for n in range(2):
        own_copies[n].wait()
        lax.fori_loop(n * n_half, (n + 1) * n_half, near_half(own, c, 0), 0)
    pl.semaphore_wait(ready.at[0], 2 + n_near)
    if n_hi > 3:
        greet(ready.at[1], [])
    at = pl.ds(pl.multiple_of(c * pair, pair), pair)
    v, u = stacked(jnp.concatenate([lhi[at, :], llo[at, :]], axis=0), lhi[at, :])
    diag[hi, c, 0:pair, :] = v + (u + u.T)
    for n in range(1, n_hi - 2):
        pl.semaphore_wait(ready.at[n], n_near)
        if n < n_hi - 3:
            greet(ready.at[n + 1], [])
    ref = diag.at[hi, c, pl.ds(0, pair)]
    dz = [remote(ref, ref, dz_s.at[d - 1], dz_r.at[d - 1], z_peer(d)) for d in range(1, n_hi)]

    id_copies[0].wait()
    weights(y * 2 + 1 - c, 2)
    for n in range(2):
        par_copies[n].wait()
        lax.fori_loop(n * n_half, (n + 1) * n_half, near_half(par, 1 - c, 2), 0)
    at = pl.ds(pl.multiple_of(c * blk, blk), blk)
    right = slice(pair, 2 * pair)
    v, u = stacked(jnp.concatenate([lhi[at, :], llo[at, :]], axis=0), lhi[right, :])
    diag[hi, c, pair:pair + blk, :] = v + u + dot(lhi[at, :], llo[right, :], NT)
    ref = diag.at[hi, c, pl.ds(pair, blk)]
    dz += [remote(ref, ref, cz_s.at[d - 1], cz_r.at[d - 1], z_peer(d)) for d in range(1, n_hi)]

    id_copies[1].wait()
    theirs = ids.at[hi, (1 - y) * 2 + c]
    remote(theirs, theirs, ids_s.at[2], ids_r.at[2], partner).wait()
    ref = ids.at[hi]
    idz = [remote(ref, ref, idz_s.at[d - 1], idz_r.at[d - 1], z_peer(d)) for d in range(1, n_hi)]
    weights((1 - y) * 2 + c, 4)
    near_q = pl.ds(pl.multiple_of(y * far_q * n_orb, LANES), far_q * n_orb)

    def chunk_at(j):
        first, width = spans[j]
        return slice(4 * first, 4 * (first + width))

    def stream(j):
        first, width = spans[j]
        part, tall = 4 * width, 2 * width
        y_copies[j].wait()
        rows = jnp.concatenate([rx[q, 2 * first:2 * first + tall, :] for q in range(far_q)], axis=0)
        res = [transform(rows, 4 + s) for s in range(2)]
        even = lax.rem(lax.broadcasted_iota(jnp.int32, (tall, n_orb), 0), 2) == 0
        for q in range(far_q):
            at = slice(q * tall, (q + 1) * tall)
            both = [jnp.where(even, res[0][at, p * n_orb:(p + 1) * n_orb], res[1][at, p * n_orb:(p + 1) * n_orb])
                    for p in range(2)]
            h, l = split(jnp.concatenate(both, axis=0))
            far[0:part, q * n_orb:(q + 1) * n_orb] = h
            far[part:2 * part, q * n_orb:(q + 1) * n_orb] = l
        v = dot(lhi[:, near_q], far[0:2 * part, :], NT).T
        off[hi, c, chunk_at(j), :] = v[:part] + v[part:] + dot(llo[:, near_q], far[0:part, :], NT).T
        ref = off.at[hi, c, pl.ds(4 * first, part)]
        return [remote(ref, ref, oz_s.at[j, d - 1], oz_r.at[j, d - 1], z_peer(d)) for d in range(1, n_hi)]

    def share(copies, ref, s, r):
        for cp in copies:
            cp.wait()
        return remote(ref, ref, s, r, partner)

    def share_off(j):
        return share(oz[j], off.at[:, c, pl.ds(4 * spans[j][0], 4 * spans[j][1])], od_s.at[j], od_r.at[j])

    def onehot(pos, where):
        return (pos == where).astype(jnp.float32).astype(jnp.bfloat16)

    n_row = 2 * out_rows

    def positions(n):
        r = lax.broadcasted_iota(jnp.int32, (n_row, n), 0)
        r = jnp.where(r < out_rows, r + (1 - lo) * out_rows, r - (1 - lo) * out_rows) + hi * n_row
        col = lax.broadcasted_iota(jnp.int32, (out_cols, n), 0)
        return [r] + [col + (h * 2 + c) * out_cols for h in (1 - y, y)]

    def lanes_of(j):
        first, width = spans[j]
        return slice(n_hi * 8 * first, n_hi * 8 * (first + width))

    def place_ids():
        sides = [slice(0, n_row)] + [slice(n_row + h * out_cols, n_row + (h + 1) * out_cols) for h in range(2)]
        pos = positions(2 * pair)
        for g in range(n_hi):
            where = jnp.concatenate([ids[g, y * 2 + e, 2:3, :] for e in range(2)], axis=1)
            for span, at in zip(sides, pos):
                p_l[g, span, :] = onehot(at, where)
        for j in range(STREAM):
            where = jnp.concatenate([ids[g, (1 - y) * 2 + e, 3:4, chunk_at(j)]
                                     for g in range(n_hi) for e in range(2)], axis=1)
            for side, at in zip(sides, positions(where.shape[1])):
                p_f[side, lanes_of(j)] = onehot(at, where)

    def expand_diag():
        total = [None, None]
        for g in range(n_hi):
            rows = [p_l[g, 0:n_row, e * pair:(e + 1) * pair] for e in range(2)]
            cross = jnp.concatenate([diag[g, e, pair:pair + blk, :] for e in range(2)], axis=0)
            t = [None, None]
            for e in range(2):
                for v in split(diag[g, e, 0:pair, :]):
                    v = dot(rows[e], v, NN)
                    t[e] = v if t[e] is None else t[e] + v
            for v in split(cross):
                t[1] = t[1] + dot(rows[0], v, NN)
                t[0] = t[0] + dot(rows[1], v, NT)
            for v in split(jnp.concatenate(t, axis=1)):
                for h in range(2):
                    u = dot(v, p_l[g, n_row + h * out_cols:n_row + (h + 1) * out_cols, :], NT)
                    total[h] = u if total[h] is None else total[h] + u
        for h in range(2):
            for x in range(2):
                acc[x, h] = total[h][x * out_rows:(x + 1) * out_rows, :]

    def spread(j):
        rows, cols = [], [[], []]
        for g in range(n_hi):
            v = jnp.concatenate(split(jnp.concatenate([off[g, e, chunk_at(j), :] for e in range(2)], axis=0)), axis=0)
            v = dot(v, p_l[g], NT)
            n = v.shape[0] // 2
            v = v[:n] + v[n:]
            rows.append(v[:, 0:n_row])
            for h in range(2):
                cols[h].append(v[:, n_row + h * out_cols:n_row + (h + 1) * out_cols])
        rows = jnp.concatenate(rows, axis=0).T
        return (split(rows), [split(jnp.concatenate(v, axis=0)) for v in cols])

    def expand_off(j, after):
        rows, cols = spread(j)
        pick = p_f[0:n_row, lanes_of(j)]
        for h in range(2):
            v = dot(pick, cols[h][0], NN) + dot(pick, cols[h][1], NN)
            there = p_f[n_row + h * out_cols:n_row + (h + 1) * out_cols, lanes_of(j)]
            v = v + dot(rows[0], there, NT) + dot(rows[1], there, NT)
            for x in range(2):
                acc[x, h] += v[x * out_rows:(x + 1) * out_rows, :]
            after(h)

    def later(h):
        pass

    oz, od = [], []
    oz.append(stream(0))
    for cp in idz:
        cp.wait()
    place_ids()
    oz.append(stream(1))
    dd = share(dz, diag.at[:, c], dd_s, dd_r)
    oz.append(stream(2))
    od.append(share_off(0))
    dd.wait()
    expand_diag()
    oz.append(stream(3))
    od.append(share_off(1))
    od[0].wait()
    expand_off(0, later)
    od.append(share_off(2))
    for j in range(1, STREAM - 1):
        od[j].wait()
        expand_off(j, later)
    od.append(share_off(STREAM - 1))
    od[STREAM - 1].wait()
    sends = []

    def send(n, x, h):
        sends.append(remote(acc.at[x, h], acc_in.at[n], xy_s.at[n], xy_r.at[n], others[n]))

    def finish(h):
        send(h, 0, h)
        if h == 0:
            send(2, 1, 0)

    expand_off(STREAM - 1, finish)
    out[0] = acc[1, 1]
    for cp in sends:
        cp.wait()
    out[1] = acc_in[0] + acc_in[1] + acc_in[2]


def stream_call(n_hi, tiles, pair_list, pair_count, orbitals, out_rows, out_cols):
    n_q, rows2, _ = tiles.shape
    n_orb, _ = orbitals.shape
    krows = rows2 // 2
    far_q, blk, pair = n_q // 2, 2 * krows, 4 * krows
    part = max(4 * width for _, width in chunks(krows))
    n_pos = 2 * out_rows + 2 * out_cols
    f32, bf16, dma, vmem = jnp.float32, jnp.bfloat16, pltpu.SemaphoreType.DMA, pltpu.VMEM
    z = n_hi - 1
    sems = [(2,)] * 4 + [(STREAM,)] * 2 + [(3,)] * 2 + [(z,)] * 6 + [()] * 2 + [(STREAM, z)] * 2 + [(STREAM,)] * 2
    sems += [(3,)] * 2
    return pl.pallas_call(
        functools.partial(stream_kernel, n_hi),
        name="exchange",
        out_shape=jax.ShapeDtypeStruct((2, out_rows, out_cols), f32),
        in_specs=[pl.BlockSpec(memory_space=space) for space in (pl.ANY, pl.ANY, pltpu.SMEM, pl.ANY)],
        out_specs=pl.BlockSpec(memory_space=vmem),
        scratch_shapes=[
            pltpu.SMEM(pair_list.shape, jnp.int32),
            vmem(orbitals.shape, f32),
            vmem(tiles.shape, f32),
            vmem(tiles.shape, f32),
            vmem((far_q, 2 * krows, LANES), f32),
            vmem((n_hi, 4, 8, LANES), jnp.int32),
            vmem((6, 2 * n_orb, 3 * LANES), bf16),
            vmem((2 * pair, n_q * n_orb), bf16),
            vmem((2 * pair, n_q * n_orb), bf16),
            vmem((2 * part, far_q * n_orb), bf16),
            vmem((n_hi, 2, pair + blk, LANES), f32),
            vmem((n_hi, 2, pair, 2 * pair), f32),
            vmem((n_hi, n_pos, 2 * pair), bf16),
            vmem((n_pos, n_hi * 2 * pair), bf16),
            vmem((2, 2, out_rows, out_cols), f32),
            vmem((3, out_rows, out_cols), f32),
        ] + [dma(s) for s in sems] + [pltpu.SemaphoreType.REGULAR((max(n_hi - 2, 1),))],
        compiler_params=pltpu.CompilerParams(collective_id=0, has_side_effects=True),
    )(tiles, pair_list, pair_count, orbitals)


def per_device(n_aux, n_occ, blocks, pair_list, pair_count, orbitals):
    n_q, slots, area = blocks.shape
    n_orb, nbf = orbitals.shape
    krows = area // LANES
    blk = 2 * krows
    tiles = blocks.reshape(n_q, slots, krows, LANES).transpose(0, 2, 1, 3).reshape(n_q, krows * slots, LANES)
    if n_occ == 4 and slots * blk == LANES:
        sums = stream_call(n_aux // 2, tiles, pair_list, pair_count, orbitals, nbf // n_aux, nbf // n_occ)
        return sums[0] + sums[1]
    own_q = n_q // n_occ
    n_sub = math.gcd(own_q, 6)
    sub_k = own_q // n_sub * n_orb
    compact = slots * n_occ * blk
    side = 2 * slots * blk
    n_y, n_hi = n_occ // 2, n_aux // 2
    off_rows = n_y * (n_y - 1) // 2 * side
    out_rows, out_cols = nbf // n_aux, nbf // n_occ
    f32, bf16, dma, vmem = jnp.float32, jnp.bfloat16, pltpu.SemaphoreType.DMA, pltpu.VMEM
    sems = [(2,), (n_y,)] + [(n_sub, n_occ)] * 2 + [(n_y,)] * 2 + [(n_occ - 1,)] * 2 + [()] * 6 + [(n_y,)] * 4
    sems += [()] * 4 + [(PIECES, n_y - 1)] * 2 + [(PIECES,)] * 6 + [(n_hi - 1,)] * 2
    sums = pl.pallas_call(
        functools.partial(kernel, n_aux, n_occ, n_sub),
        name="exchange",
        out_shape=jax.ShapeDtypeStruct((2, out_rows, out_cols), f32),
        in_specs=[pl.BlockSpec(memory_space=space) for space in (pl.ANY, pl.ANY, pltpu.SMEM, pl.ANY)],
        out_specs=pl.BlockSpec(memory_space=vmem),
        scratch_shapes=[
            pltpu.SMEM(pair_list.shape, jnp.int32),
            vmem(orbitals.shape, f32),
            vmem((n_occ, own_q, krows * slots, LANES), f32),
            vmem((2, n_y - 1, own_q, krows * slots, LANES), f32),
            vmem((2, n_occ, 8, LANES), jnp.int32),
            vmem((slots * n_occ, 2 * n_orb, 2 * LANES), bf16),
            vmem((slots * n_occ, 2 * n_orb, LANES), bf16),
            vmem((compact, own_q * n_orb), bf16),
            vmem((compact, own_q * n_orb), bf16),
            vmem((side, sub_k), bf16),
            vmem((side, sub_k), bf16),
            vmem((side, side), f32),
            vmem((side // 2, side), f32),
            vmem((2, n_y, side, side), f32),
            vmem((off_rows, side), f32),
            vmem((off_rows // 2, side), f32),
            vmem((off_rows // 2, side), f32),
            vmem((n_y - 1, off_rows // 2, side), f32),
            vmem((2, off_rows, side), f32),
            vmem((n_hi - 1, out_rows, out_cols), f32),
            vmem((n_hi - 1, out_rows, out_cols), f32),
        ] + [dma(s) for s in sems],
        compiler_params=pltpu.CompilerParams(collective_id=0, has_side_effects=True),
    )(tiles, pair_list, pair_count, orbitals)
    return sums[0] + sums[1]


def solution(mesh):
    body = functools.partial(per_device, mesh.shape["aux"], mesh.shape["occ"])
    in_specs = (P("aux", "occ", None), P("aux", "occ", None), P("aux"), P())
    return jax.shard_map(body, mesh=mesh, in_specs=in_specs, out_specs=P("aux", "occ"), check_vma=False)
```

```python
import functools
import math

import jax
import jax.numpy as jnp
from jax import lax
from jax.experimental import pallas as pl
from jax.experimental.pallas import tpu as pltpu
from jax.sharding import PartitionSpec as P

LANES = 128
PIECES = 2
MESH = pl.DeviceIdType.MESH
NT = (((1,), (1,)), ((), ()))
NN = (((1,), (0,)), ((), ()))


def dot(a, b, dims):
    return lax.dot_general(a, b, dims, preferred_element_type=jnp.float32)


def split(x):
    hi = x.astype(jnp.bfloat16)
    return hi, (x - hi.astype(jnp.float32)).astype(jnp.bfloat16)


def kernel(n_aux, n_occ, n_sub, tiles, pairs_hbm, count_in, orb_hbm, out, pairs_in, orb, rx, rxd, ids, whi, wlo, hhi, hlo,
           dhi, dlo, diag, dcore, dfull, off, ocore, opair, oin, ofull, dense, z_in,
           in_s, local_s, tile_s, tile_r, quart_s, quart_r, ids_s, ids_r, idx_s, idx_r, dc_s, dc_r,
           dx_s, dx_r, dy_s, dy_r, df_s, df_r, dd_s, dd_r, oc_s, oc_r, oy_s, oy_r, ox_s, ox_r,
           op_s, op_r, of_s, of_r, z_s, z_r):
    a, o = lax.axis_index("aux"), lax.axis_index("occ")
    n_y, n_hi = n_occ // 2, n_aux // 2
    y, c = o // 2, lax.rem(o, 2)
    hi_a, lo = a // 2, lax.rem(a, 2)
    own_q = tiles.shape[0] // n_occ
    sub_q = own_q // n_sub
    krows = tiles.shape[1] // 2
    blk = 2 * krows
    side = 4 * blk
    n_slots = 2 * n_occ
    n_off = n_y * (n_y - 1) // 2
    d_half, o_half = side // 2, n_off * side // 2
    piece = o_half // PIECES
    nbf, n_orb = orb.shape[1], orb.shape[0]

    def y_peer(d):
        return lax.rem(y + d, n_y)

    peers = [(d, e) for d in range(1, n_y) for e in (0, 1)] + [(0, 1)]

    def occ_peer(d, e):
        return y_peer(d) * 2 + (c if e == 0 else 1 - c)

    partner = (a, occ_peer(0, 1))
    x_peer = (a + 1 - 2 * lo, o)

    def z_peer(d):
        return (lax.rem(hi_a + d, n_hi) * 2 + lo, o)

    barrier = pltpu.get_barrier_semaphore()
    greet = [(a, occ_peer(*d)) for d in peers] + [x_peer] + [z_peer(d) for d in range(1, n_hi)]
    for dev in greet:
        pl.semaphore_signal(barrier, inc=1, device_id=dev, device_id_type=MESH)

    def local(src, dst, s):
        cp = pltpu.make_async_copy(src, dst, s)
        cp.start()
        return cp

    def quarter(index):
        return tiles.at[pl.ds(index * own_q, own_q)]

    inputs = [local(src, dst, in_s.at[n]) for n, (src, dst) in enumerate(
        ((pairs_hbm, pairs_in), (orb_hbm, orb)))]
    locals_ = [local(quarter(o), rx.at[o], local_s.at[0])]
    for d in range(1, n_y):
        locals_.append(local(quarter(y_peer(d) * 2 + c), rxd.at[c, d - 1], local_s.at[d]))
    pl.semaphore_wait(barrier, len(greet))

    def remote(src, dst, s, r, dev):
        cp = pltpu.make_async_remote_copy(
            src_ref=src, dst_ref=dst, send_sem=s, recv_sem=r, device_id=dev, device_id_type=MESH
        )
        cp.start()
        return cp

    def sub_tiles(j, d, e):
        peer = occ_peer(d, e)
        n = d * 2 + e
        return remote(tiles.at[pl.ds(peer * own_q + j * sub_q, sub_q)], rx.at[o, pl.ds(j * sub_q, sub_q)],
                      tile_s.at[j, n], tile_r.at[j, n], (a, peer))

    def tiles_of(j):
        return [sub_tiles(j, d, e) for d in range(1, n_y) for e in (0, 1)]

    tile_copies = [tiles_of(0)]
    quarters = []
    inputs[0].wait()
    lane1 = lax.broadcasted_iota(jnp.int32, (8, LANES), 1)
    row1 = lax.broadcasted_iota(jnp.int32, (8, LANES), 0)
    within = lax.rem(lane1, blk)
    place = lax.rem(within, krows) * 2 + within // krows
    live = [jnp.where(o * 2 + s < count_in[0], pairs_in[0, s, 0] * blk, -nbf - blk) for s in range(2)]
    cols = jnp.where(row1 == 0, pairs_in[0, 0, 1], pairs_in[0, 1, 1]) * blk + within
    ids[lo, o] = jnp.where(row1 < 2, cols, jnp.where(lane1 < blk, live[0], live[1]) + place)
    id_copies = []
    for n, d in enumerate(peers):
        id_copies.append(remote(ids.at[lo, o], ids.at[lo, o], ids_s.at[n], ids_r.at[n], (a, occ_peer(*d))))
    for d in range(1, n_y):
        quarters.append(remote(quarter(y_peer(d) * 2 + 1 - c), rxd.at[c, d - 1],
                               quart_s.at[d], quart_r.at[d], partner))
    quarters.append(remote(quarter(o + 1 - 2 * c), rx.at[o], quart_s.at[0], quart_r.at[0], partner))
    for j in range(1, n_sub):
        tile_copies.append(tiles_of(j))
    inputs[1].wait()
    orb_hi, orb_lo = split(orb[...])
    row_pos = lax.broadcasted_iota(jnp.int32, (nbf, LANES), 0)
    lane = lax.broadcasted_iota(jnp.int32, (n_orb, LANES), 1)
    def weights(src):
        for s in range(2):
            sel = (row_pos == ids[lo, src, pl.ds(s, 1), :]).astype(jnp.float32).astype(jnp.bfloat16)
            for orb_part, copies, dst in ((orb_hi, 2, whi), (orb_lo, 1, wlo)):
                w = dot(orb_part, sel, NN)
                for p in range(2):
                    keep = lane < blk if p == 0 else lane >= blk
                    w_p = jnp.where(keep, w, 0.0).astype(jnp.bfloat16)
                    for n in range(copies):
                        dst[src * 2 + s, p * n_orb:(p + 1) * n_orb, n * LANES:(n + 1) * LANES] = w_p

    id_copies[-1].wait()
    for e in range(2):
        weights(y * 2 + e)

    def half(load, slot, row0, q0, hi_ref, lo_ref):
        rows = jnp.concatenate([load(q) for q in range(sub_q)], axis=0)
        bh, bl = split(rows)
        wh, wl = whi[slot], wlo[slot]
        res = dot(jnp.concatenate([bh, bl], axis=1), wh, NT) + dot(bh, wl, NT)
        for q in range(sub_q):
            for p in range(2):
                ph, pl_ = split(res[q * krows:(q + 1) * krows, p * n_orb:(p + 1) * n_orb])
                at = pl.ds(pl.multiple_of(row0 + p * krows, krows), krows)
                lanes = slice((q0 + q) * n_orb, (q0 + q + 1) * n_orb)
                hi_ref[at, lanes] = ph
                lo_ref[at, lanes] = pl_

    def gram(hi_i, lo_i, hi_k, lo_k):
        return dot(hi_i, hi_k, NT) + dot(hi_i, lo_k, NT) + dot(lo_i, hi_k, NT)

    for cp in locals_ + quarters:
        cp.wait()
    total = None
    for d in range(1, n_y):
        for j in range(n_sub):
            for e in range(2):
                for s in range(2):
                    half(lambda q: rxd[e, d - 1, j * sub_q + q, pl.ds(s, krows, stride=2), :],
                         (y * 2 + e) * 2 + s, (e * 2 + s) * blk, 0, dhi, dlo)
            val = gram(dhi[...], dlo[...], dhi[...], dlo[...])
            total = val if total is None else total + val
    mine = pl.ds(pl.multiple_of(y * side, side), side)
    for j in range(n_sub):
        for e in range(2):
            for s in range(2):
                half(lambda q: rx[y * 2 + e, j * sub_q + q, pl.ds(s, krows, stride=2), :],
                     (y * 2 + e) * 2 + s, ((y * 2 + e) * 2 + s) * blk, j * sub_q, hhi, hlo)
    total = total + gram(hhi[mine, :], hlo[mine, :], hhi[mine, :], hlo[mine, :])
    diag[...] = total
    cp = remote(diag.at[pl.ds((1 - c) * d_half, d_half)], dcore, dc_s, dc_r, partner)
    cp.wait()
    my_d = pl.ds(pl.multiple_of(c * d_half, d_half), d_half)
    dfull[lo, y, my_d, :] = diag[my_d, :] + dcore[...]
    my_diag = dfull.at[lo, y, my_d]
    dx = [remote(my_diag, my_diag, dx_s, dx_r, x_peer)]
    dys = [remote(my_diag, my_diag, dy_s.at[d], dy_r.at[d], (a, y_peer(d) * 2 + c)) for d in range(1, n_y)]

    for cp in id_copies[:-1]:
        cp.wait()
    idx_copy = remote(ids.at[lo], ids.at[lo], idx_s, idx_r, x_peer)
    for d in range(1, n_y):
        for e in range(2):
            weights(y_peer(d) * 2 + e)
    offs = [(i, k) for i in range(n_y) for k in range(i)]
    for j in range(n_sub):
        for cp in tile_copies[j]:
            cp.wait()
        for d in range(1, n_y):
            for e in range(2):
                for s in range(2):
                    src = y_peer(d) * 2 + e
                    half(lambda q: rx[src, j * sub_q + q, pl.ds(s, krows, stride=2), :],
                         src * 2 + s, (src * 2 + s) * blk, j * sub_q, hhi, hlo)
        at = slice(j * sub_q * n_orb, (j + 1) * sub_q * n_orb)
        for b, (i, k) in enumerate(offs):
            ri, rk = slice(i * side, (i + 1) * side), slice(k * side, (k + 1) * side)
            val = gram(hhi[ri, at], hlo[ri, at], hhi[rk, at], hlo[rk, at])
            if j:
                val = val + off[b * side:(b + 1) * side, :]
            off[b * side:(b + 1) * side, :] = val
    cp = remote(off.at[pl.ds((1 - c) * o_half, o_half)], ocore, oc_s, oc_r, partner)
    cp.wait()
    opair[...] = off[pl.ds(pl.multiple_of(c * o_half, piece), o_half), :] + ocore[...]
    oys = []
    for p in range(PIECES):
        at = pl.ds(p * piece, piece)
        oys.append([remote(opair.at[at], oin.at[d - 1, at], oy_s.at[p, d - 1], oy_r.at[p, d - 1],
                           (a, y_peer(d) * 2 + c)) for d in range(1, n_y)])
    dfs = []
    for d in range(1, n_y):
        dys[d - 1].wait_recv()
        got = dfull.at[lo, y_peer(n_y - d), my_d]
        dfs.append(remote(got, got, df_s.at[d], df_r.at[d], x_peer))
    oxs, ops = [], []
    for p in range(PIECES):
        val = opair[p * piece:(p + 1) * piece, :]
        for d in range(1, n_y):
            oys[p][d - 1].wait()
            val = val + oin[d - 1, p * piece:(p + 1) * piece, :]
        at = pl.ds(pl.multiple_of(c * o_half + p * piece, piece), piece)
        ofull[lo, at, :] = val
        ref = ofull.at[lo, at]
        oxs.append(remote(ref, ref, ox_s.at[p], ox_r.at[p], x_peer))
        ops.append(remote(ref, ref, op_s.at[p], op_r.at[p], partner))
    for cp in dx + dfs:
        cp.wait()
    for cp in dys:
        cp.wait_send()
    idx_copy.wait()
    half_d = dfull.at[:, :, my_d]
    cp = remote(half_d, half_d, dd_s, dd_r, partner)

    out_rows, out_cols = out.shape[1:]
    compact = n_slots * blk
    col_pos = lax.broadcasted_iota(jnp.int32, (out_cols, compact), 0) + o * out_cols
    row_i = lax.broadcasted_iota(jnp.int32, (n_hi * out_rows, compact), 0)
    row_h = lax.rem(row_i // out_rows + 1 + hi_a, n_hi)
    row_pos = (row_h * 2 + lo) * out_rows + lax.rem(row_i, out_rows)
    picks = []
    for l in range(2):
        where = jnp.concatenate([ids[l, s, 2:3, :] for s in range(n_occ)], axis=1)
        picks.append([(pos == where).astype(jnp.float32).astype(jnp.bfloat16) for pos in (col_pos, row_pos)])

    def spread(acc, l, i, t):
        for e in split(t):
            v = dot(picks[l][1][:, i * side:(i + 1) * side], e, NN)
            acc = v if acc is None else acc + v
        return acc

    cp.wait()
    acc = None
    for l in range(2):
        for i in range(n_y):
            dh, dl = split(dfull[l, i])
            cols = picks[l][0][:, i * side:(i + 1) * side]
            acc = spread(acc, l, i, dot(dh, cols, NT) + dot(dl, cols, NT))
    fwd = []
    for p in range(PIECES):
        oxs[p].wait()
        ref = ofull.at[1 - lo, pl.ds(pl.multiple_of(c * o_half + p * piece, piece), piece)]
        fwd.append(remote(ref, ref, of_s.at[p], of_r.at[p], partner))
    for cp in ops + fwd:
        cp.wait()
    parts = []
    for l in range(2):
        t = [None] * n_y
        for b, (i, k) in enumerate(offs):
            for e in split(ofull[l, b * side:(b + 1) * side, :]):
                vi = dot(e, picks[l][0][:, k * side:(k + 1) * side], NT)
                vk = dot(e, picks[l][0][:, i * side:(i + 1) * side], (((0,), (1,)), ((), ())))
                t[i] = vi if t[i] is None else t[i] + vi
                t[k] = vk if t[k] is None else t[k] + vk
        parts.append([split(v) for v in t])
    zs = []
    for g in range(n_hi // 2):
        rows = slice(2 * g * out_rows, 2 * (g + 1) * out_rows)
        v = acc[rows, :]
        for l in range(2):
            for i in range(n_y):
                for e in parts[l][i]:
                    v = v + dot(picks[l][1][rows, i * side:(i + 1) * side], e, NN)
        for n in range(2):
            d = 2 * g + n + 1
            if d < n_hi:
                dense[d - 1] = v[n * out_rows:(n + 1) * out_rows, :]
                zs.append(remote(dense.at[d - 1], z_in.at[d - 1], z_s.at[d - 1], z_r.at[d - 1], z_peer(d)))
            else:
                out[0] = v[n * out_rows:(n + 1) * out_rows, :]
    result = None
    for d in range(1, n_hi):
        zs[d - 1].wait()
        result = z_in[d - 1] if result is None else result + z_in[d - 1]
    out[1] = result


SHARES = (3, 2, 2, 1)
STREAM = len(SHARES)


def chunks(krows):
    unit, first = krows // sum(SHARES), 0
    spans = []
    for share in SHARES:
        spans.append((first * unit, share * unit))
        first += share
    return spans


def stream_kernel(n_hi, tiles, pairs_hbm, count_in, orb_hbm, out, pairs_in, orb, own, par, rx, ids, w_all, lhi, llo,
                  far, diag, off, p_l, p_f, acc, acc_in, in_s, own_s, par_s, par_r, y_s, y_r, ids_s, ids_r,
                  idz_s, idz_r, dz_s, dz_r, cz_s, cz_r, dd_s, dd_r, oz_s, oz_r, od_s, od_r, xy_s, xy_r, ready):
    a, o = lax.axis_index("aux"), lax.axis_index("occ")
    hi, lo, y, c = a // 2, lax.rem(a, 2), o // 2, lax.rem(o, 2)
    n_q, krows = tiles.shape[0], tiles.shape[1] // 2
    far_q, spans = n_q // 2, chunks(krows)
    blk, pair = 2 * krows, 4 * krows
    n_orb, nbf = orb.shape
    out_rows, out_cols = out.shape[1:]
    partner = (a, y * 2 + 1 - c)
    across = (a, (1 - y) * 2 + c)
    x_peer = (hi * 2 + 1 - lo, o)
    others = [(hi * 2 + 1 - lo, (1 - y) * 2 + c), x_peer, across]

    def z_peer(d):
        return (lax.rem(hi + d, n_hi) * 2 + lo, o)

    barrier = pltpu.get_barrier_semaphore()
    n_near = jnp.where(hi > 0, 1, 0) + jnp.where(hi < n_hi - 1, 1, 0)

    def greet(sem, devices):
        for dev in devices:
            pl.semaphore_signal(sem, inc=1, device_id=dev, device_id_type=MESH)

        @pl.when(hi > 0)
        def _():
            pl.semaphore_signal(sem, inc=1, device_id=(a - 2, o), device_id_type=MESH)

        @pl.when(hi < n_hi - 1)
        def _():
            pl.semaphore_signal(sem, inc=1, device_id=(a + 2, o), device_id_type=MESH)

    greet(barrier, [partner, across, x_peer])

    def local(src, dst, s):
        cp = pltpu.make_async_copy(src, dst, s)
        cp.start()
        return cp

    def remote(src, dst, s, r, dev):
        cp = pltpu.make_async_remote_copy(
            src_ref=src, dst_ref=dst, send_sem=s, recv_sem=r, device_id=dev, device_id_type=MESH
        )
        cp.start()
        return cp

    inputs = [local(src, dst, in_s.at[n]) for n, (src, dst) in enumerate(
        ((pairs_hbm, pairs_in), (orb_hbm, orb)))]
    halves = [pl.ds(n * far_q, far_q) for n in range(2)]
    own_copies = [local(tiles.at[h], own.at[h], own_s.at[n]) for n, h in enumerate(halves)]

    inputs[0].wait()
    lane1 = lax.broadcasted_iota(jnp.int32, (8, LANES), 1)
    row1 = lax.broadcasted_iota(jnp.int32, (8, LANES), 0)
    within = lax.rem(lane1, blk)
    place = lax.rem(within, krows) * 2 + within // krows
    live = [jnp.where(o * 2 + s < count_in[0], pairs_in[0, s, 0] * blk, -nbf - blk) for s in range(2)]
    cols = jnp.where(row1 == 0, pairs_in[0, 0, 1], pairs_in[0, 1, 1]) * blk + within
    near = jnp.where(lane1 < blk, live[0], live[1]) + place
    far_id = jnp.zeros((8, LANES), jnp.int32)
    for first, width in spans:
        at = lane1 - 4 * first
        tile_row = first * 2 + lax.rem(at, 2 * width)
        spot = jnp.where(lax.rem(tile_row, 2) == 0, live[0], live[1]) + tile_row // 2 * 2 + at // (2 * width)
        far_id = jnp.where((at >= 0) & (at < 4 * width), spot, far_id)
    ids[hi, o] = jnp.where(row1 < 2, cols, jnp.where(row1 == 2, near, far_id))

    pl.semaphore_wait(barrier, 3 + n_near)
    mine = ids.at[hi, o]

    id_copies = [remote(mine, mine, ids_s.at[n], ids_r.at[n], dev) for n, dev in enumerate((partner, across))]
    far_rows = pl.ds(pl.multiple_of((1 - y) * far_q, far_q), far_q)
    y_copies = [remote(tiles.at[far_rows, pl.ds(2 * first, 2 * width)], rx.at[:, pl.ds(2 * first, 2 * width)],
                       y_s.at[j], y_r.at[j], across) for j, (first, width) in enumerate(spans)]
    par_copies = [remote(tiles.at[h], par.at[h], par_s.at[n], par_r.at[n], partner) for n, h in enumerate(halves)]
    greet(ready.at[0], [partner, x_peer])
    inputs[1].wait()
    orb_hi, orb_lo = split(orb[...])
    row_pos = lax.broadcasted_iota(jnp.int32, (nbf, LANES), 0)
    lane = lax.broadcasted_iota(jnp.int32, (n_orb, LANES), 1)

    def weights(src, base):
        for s in range(2):
            sel = (row_pos == ids[hi, src, pl.ds(s, 1), :]).astype(jnp.float32).astype(jnp.bfloat16)
            for orb_part, spots in ((orb_hi, (0, 1)), (orb_lo, (2,))):
                w = dot(orb_part, sel, NN)
                for p in range(2):
                    keep = lane < blk if p == 0 else lane >= blk
                    w_p = jnp.where(keep, w, 0.0).astype(jnp.bfloat16)
                    for n in spots:
                        w_all[base + s, p * n_orb:(p + 1) * n_orb, n * LANES:(n + 1) * LANES] = w_p

    def transform(rows, slot):
        bh, bl = split(rows)
        return dot(jnp.concatenate([bh, bl, bh], axis=1), w_all[slot], NT)

    batch = math.gcd(far_q, 8)

    def near_half(src, e, base):
        def step(b, carry):
            for s in range(2):
                res = transform(jnp.concatenate(
                    [src[b * batch + q, pl.ds(s, krows, stride=2), :] for q in range(batch)], axis=0), base + s)
                for q in range(batch):
                    lanes = pl.ds(pl.multiple_of((b * batch + q) * n_orb, n_orb), n_orb)
                    for p in range(2):
                        h, l = split(res[q * krows:(q + 1) * krows, p * n_orb:(p + 1) * n_orb])
                        at = pl.ds(pl.multiple_of(e * pair + s * blk + p * krows, krows), krows)
                        lhi[at, lanes] = h
                        llo[at, lanes] = l
            return carry
        return step

    def stacked(both, hi_k):
        v = dot(both, hi_k, NT)
        n = v.shape[0] // 2
        return v[:n], v[n:]

    n_half = far_q // batch
    weights(o, 0)

    for n in range(2):
        own_copies[n].wait()
        lax.fori_loop(n * n_half, (n + 1) * n_half, near_half(own, c, 0), 0)
    pl.semaphore_wait(ready.at[0], 2 + n_near)
    if n_hi > 3:
        greet(ready.at[1], [])
    at = pl.ds(pl.multiple_of(c * pair, pair), pair)
    v, u = stacked(jnp.concatenate([lhi[at, :], llo[at, :]], axis=0), lhi[at, :])
    v = v + (u + u.T)
    diag[hi, c, 0:blk, :] = v[:blk]
    diag[hi, c, blk:pair - krows, :] = jnp.concatenate([v[blk:blk + krows, blk:], v[blk + krows:, blk:]], axis=1)
    for n in range(1, n_hi - 2):
        pl.semaphore_wait(ready.at[n], n_near)
        if n < n_hi - 3:
            greet(ready.at[n + 1], [])
    ref = diag.at[hi, c, pl.ds(0, pair - krows)]
    dz = [remote(ref, ref, dz_s.at[d - 1], dz_r.at[d - 1], z_peer(d)) for d in range(1, n_hi)]

    id_copies[0].wait()
    weights(y * 2 + 1 - c, 2)
    for n in range(2):
        par_copies[n].wait()
        lax.fori_loop(n * n_half, (n + 1) * n_half, near_half(par, 1 - c, 2), 0)
    at = pl.ds(pl.multiple_of(c * blk, blk), blk)
    right = slice(pair, 2 * pair)
    v, u = stacked(jnp.concatenate([lhi[at, :], llo[at, :]], axis=0), lhi[right, :])
    diag[hi, c, pair - krows:pair + krows, :] = v + u + dot(lhi[at, :], llo[right, :], NT)
    ref = diag.at[hi, c, pl.ds(pair - krows, blk)]
    dz += [remote(ref, ref, cz_s.at[d - 1], cz_r.at[d - 1], z_peer(d)) for d in range(1, n_hi)]

    id_copies[1].wait()
    theirs = ids.at[hi, (1 - y) * 2 + c]
    remote(theirs, theirs, ids_s.at[2], ids_r.at[2], partner).wait()
    ref = ids.at[hi]
    idz = [remote(ref, ref, idz_s.at[d - 1], idz_r.at[d - 1], z_peer(d)) for d in range(1, n_hi)]
    weights((1 - y) * 2 + c, 4)
    near_q = pl.ds(pl.multiple_of(y * far_q * n_orb, LANES), far_q * n_orb)

    def chunk_at(j):
        first, width = spans[j]
        return slice(4 * first, 4 * (first + width))

    def stream(j):
        first, width = spans[j]
        part, tall = 4 * width, 2 * width
        y_copies[j].wait()
        rows = jnp.concatenate([rx[q, 2 * first:2 * first + tall, :] for q in range(far_q)], axis=0)
        res = [transform(rows, 4 + s) for s in range(2)]
        even = lax.rem(lax.broadcasted_iota(jnp.int32, (tall, n_orb), 0), 2) == 0
        for q in range(far_q):
            at = slice(q * tall, (q + 1) * tall)
            both = [jnp.where(even, res[0][at, p * n_orb:(p + 1) * n_orb], res[1][at, p * n_orb:(p + 1) * n_orb])
                    for p in range(2)]
            h, l = split(jnp.concatenate(both, axis=0))
            far[0:part, q * n_orb:(q + 1) * n_orb] = h
            far[part:2 * part, q * n_orb:(q + 1) * n_orb] = l
        v = dot(lhi[:, near_q], far[0:2 * part, :], NT).T
        off[hi, c, chunk_at(j), :] = v[:part] + v[part:] + dot(llo[:, near_q], far[0:part, :], NT).T
        ref = off.at[hi, c, pl.ds(4 * first, part)]
        return [remote(ref, ref, oz_s.at[j, d - 1], oz_r.at[j, d - 1], z_peer(d)) for d in range(1, n_hi)]

    def share(copies, ref, s, r):
        for cp in copies:
            cp.wait()
        return remote(ref, ref, s, r, partner)

    def share_off(j):
        return share(oz[j], off.at[:, c, pl.ds(4 * spans[j][0], 4 * spans[j][1])], od_s.at[j], od_r.at[j])

    def onehot(pos, where):
        return (pos == where).astype(jnp.float32).astype(jnp.bfloat16)

    n_row = 2 * out_rows

    def positions(n):
        r = lax.broadcasted_iota(jnp.int32, (n_row, n), 0)
        r = jnp.where(r < out_rows, r + (1 - lo) * out_rows, r - (1 - lo) * out_rows) + hi * n_row
        col = lax.broadcasted_iota(jnp.int32, (out_cols, n), 0)
        return [r] + [col + (h * 2 + c) * out_cols for h in (1 - y, y)]

    def lanes_of(j):
        first, width = spans[j]
        return slice(n_hi * 8 * first, n_hi * 8 * (first + width))

    def place_ids():
        sides = [slice(0, n_row)] + [slice(n_row + h * out_cols, n_row + (h + 1) * out_cols) for h in range(2)]
        pos = positions(2 * pair)
        for g in range(n_hi):
            where = jnp.concatenate([ids[g, y * 2 + e, 2:3, :] for e in range(2)], axis=1)
            for span, at in zip(sides, pos):
                p_l[g, span, :] = onehot(at, where)
        for j in range(STREAM):
            where = jnp.concatenate([ids[g, (1 - y) * 2 + e, 3:4, chunk_at(j)]
                                     for g in range(n_hi) for e in range(2)], axis=1)
            for side, at in zip(sides, positions(where.shape[1])):
                p_f[side, lanes_of(j)] = onehot(at, where)

    def expand_diag():
        total = [None, None]
        for g in range(n_hi):
            rows = [p_l[g, 0:n_row, e * pair:(e + 1) * pair] for e in range(2)]
            cross = jnp.concatenate([diag[g, e, pair - krows:pair + krows, :] for e in range(2)], axis=0)
            t = [None, None]
            for e in range(2):
                top, low = diag[g, e, 0:blk, :], diag[g, e, blk:pair - krows, :]
                low = jnp.concatenate([low[:, :blk], low[:, blk:]], axis=0)
                both = jnp.concatenate([top, jnp.concatenate([top[:, blk:].T, low], axis=1)], axis=0)
                for v in split(both):
                    v = dot(rows[e], v, NN)
                    t[e] = v if t[e] is None else t[e] + v
            for v in split(cross):
                t[1] = t[1] + dot(rows[0], v, NN)
                t[0] = t[0] + dot(rows[1], v, NT)
            for v in split(jnp.concatenate(t, axis=1)):
                for h in range(2):
                    u = dot(v, p_l[g, n_row + h * out_cols:n_row + (h + 1) * out_cols, :], NT)
                    total[h] = u if total[h] is None else total[h] + u
        for h in range(2):
            for x in range(2):
                acc[x, h] = total[h][x * out_rows:(x + 1) * out_rows, :]

    def spread(j):
        rows, cols = [], [[], []]
        for g in range(n_hi):
            v = jnp.concatenate(split(jnp.concatenate([off[g, e, chunk_at(j), :] for e in range(2)], axis=0)), axis=0)
            v = dot(v, p_l[g], NT)
            n = v.shape[0] // 2
            v = v[:n] + v[n:]
            rows.append(v[:, 0:n_row])
            for h in range(2):
                cols[h].append(v[:, n_row + h * out_cols:n_row + (h + 1) * out_cols])
        rows = jnp.concatenate(rows, axis=0).T
        return (split(rows), [split(jnp.concatenate(v, axis=0)) for v in cols])

    def expand_off(j, after):
        rows, cols = spread(j)
        pick = p_f[0:n_row, lanes_of(j)]
        for h in range(2):
            v = dot(pick, cols[h][0], NN) + dot(pick, cols[h][1], NN)
            there = p_f[n_row + h * out_cols:n_row + (h + 1) * out_cols, lanes_of(j)]
            v = v + dot(rows[0], there, NT) + dot(rows[1], there, NT)
            for x in range(2):
                acc[x, h] += v[x * out_rows:(x + 1) * out_rows, :]
            after(h)

    def later(h):
        pass

    oz, od = [], []
    oz.append(stream(0))
    for cp in idz:
        cp.wait()
    place_ids()
    oz.append(stream(1))
    dd = share(dz, diag.at[:, c], dd_s, dd_r)
    oz.append(stream(2))
    od.append(share_off(0))
    dd.wait()
    expand_diag()
    oz.append(stream(3))
    od.append(share_off(1))
    od[0].wait()
    expand_off(0, later)
    od.append(share_off(2))
    for j in range(1, STREAM - 1):
        od[j].wait()
        expand_off(j, later)
    od.append(share_off(STREAM - 1))
    od[STREAM - 1].wait()
    sends = []

    def send(n, x, h):
        sends.append(remote(acc.at[x, h], acc_in.at[n], xy_s.at[n], xy_r.at[n], others[n]))

    def finish(h):
        send(h, 0, h)
        if h == 0:
            send(2, 1, 0)

    expand_off(STREAM - 1, finish)
    out[0] = acc[1, 1]
    for cp in sends:
        cp.wait()
    out[1] = acc_in[0] + acc_in[1] + acc_in[2]


def stream_call(n_hi, tiles, pair_list, pair_count, orbitals, out_rows, out_cols):
    n_q, rows2, _ = tiles.shape
    n_orb, _ = orbitals.shape
    krows = rows2 // 2
    far_q, blk, pair = n_q // 2, 2 * krows, 4 * krows
    part = max(4 * width for _, width in chunks(krows))
    n_pos = 2 * out_rows + 2 * out_cols
    f32, bf16, dma, vmem = jnp.float32, jnp.bfloat16, pltpu.SemaphoreType.DMA, pltpu.VMEM
    z = n_hi - 1
    sems = [(2,)] * 4 + [(STREAM,)] * 2 + [(3,)] * 2 + [(z,)] * 6 + [()] * 2 + [(STREAM, z)] * 2 + [(STREAM,)] * 2
    sems += [(3,)] * 2
    return pl.pallas_call(
        functools.partial(stream_kernel, n_hi),
        name="exchange",
        out_shape=jax.ShapeDtypeStruct((2, out_rows, out_cols), f32),
        in_specs=[pl.BlockSpec(memory_space=space) for space in (pl.ANY, pl.ANY, pltpu.SMEM, pl.ANY)],
        out_specs=pl.BlockSpec(memory_space=vmem),
        scratch_shapes=[
            pltpu.SMEM(pair_list.shape, jnp.int32),
            vmem(orbitals.shape, f32),
            vmem(tiles.shape, f32),
            vmem(tiles.shape, f32),
            vmem((far_q, 2 * krows, LANES), f32),
            vmem((n_hi, 4, 8, LANES), jnp.int32),
            vmem((6, 2 * n_orb, 3 * LANES), bf16),
            vmem((2 * pair, n_q * n_orb), bf16),
            vmem((2 * pair, n_q * n_orb), bf16),
            vmem((2 * part, far_q * n_orb), bf16),
            vmem((n_hi, 2, pair + krows, LANES), f32),
            vmem((n_hi, 2, pair, 2 * pair), f32),
            vmem((n_hi, n_pos, 2 * pair), bf16),
            vmem((n_pos, n_hi * 2 * pair), bf16),
            vmem((2, 2, out_rows, out_cols), f32),
            vmem((3, out_rows, out_cols), f32),
        ] + [dma(s) for s in sems] + [pltpu.SemaphoreType.REGULAR((max(n_hi - 2, 1),))],
        compiler_params=pltpu.CompilerParams(collective_id=0, has_side_effects=True),
    )(tiles, pair_list, pair_count, orbitals)


def per_device(n_aux, n_occ, blocks, pair_list, pair_count, orbitals):
    n_q, slots, area = blocks.shape
    n_orb, nbf = orbitals.shape
    krows = area // LANES
    blk = 2 * krows
    tiles = blocks.reshape(n_q, slots, krows, LANES).transpose(0, 2, 1, 3).reshape(n_q, krows * slots, LANES)
    if n_occ == 4 and slots * blk == LANES:
        sums = stream_call(n_aux // 2, tiles, pair_list, pair_count, orbitals, nbf // n_aux, nbf // n_occ)
        return sums[0] + sums[1]
    own_q = n_q // n_occ
    n_sub = math.gcd(own_q, 6)
    sub_k = own_q // n_sub * n_orb
    compact = slots * n_occ * blk
    side = 2 * slots * blk
    n_y, n_hi = n_occ // 2, n_aux // 2
    off_rows = n_y * (n_y - 1) // 2 * side
    out_rows, out_cols = nbf // n_aux, nbf // n_occ
    f32, bf16, dma, vmem = jnp.float32, jnp.bfloat16, pltpu.SemaphoreType.DMA, pltpu.VMEM
    sems = [(2,), (n_y,)] + [(n_sub, n_occ)] * 2 + [(n_y,)] * 2 + [(n_occ - 1,)] * 2 + [()] * 6 + [(n_y,)] * 4
    sems += [()] * 4 + [(PIECES, n_y - 1)] * 2 + [(PIECES,)] * 6 + [(n_hi - 1,)] * 2
    sums = pl.pallas_call(
        functools.partial(kernel, n_aux, n_occ, n_sub),
        name="exchange",
        out_shape=jax.ShapeDtypeStruct((2, out_rows, out_cols), f32),
        in_specs=[pl.BlockSpec(memory_space=space) for space in (pl.ANY, pl.ANY, pltpu.SMEM, pl.ANY)],
        out_specs=pl.BlockSpec(memory_space=vmem),
        scratch_shapes=[
            pltpu.SMEM(pair_list.shape, jnp.int32),
            vmem(orbitals.shape, f32),
            vmem((n_occ, own_q, krows * slots, LANES), f32),
            vmem((2, n_y - 1, own_q, krows * slots, LANES), f32),
            vmem((2, n_occ, 8, LANES), jnp.int32),
            vmem((slots * n_occ, 2 * n_orb, 2 * LANES), bf16),
            vmem((slots * n_occ, 2 * n_orb, LANES), bf16),
            vmem((compact, own_q * n_orb), bf16),
            vmem((compact, own_q * n_orb), bf16),
            vmem((side, sub_k), bf16),
            vmem((side, sub_k), bf16),
            vmem((side, side), f32),
            vmem((side // 2, side), f32),
            vmem((2, n_y, side, side), f32),
            vmem((off_rows, side), f32),
            vmem((off_rows // 2, side), f32),
            vmem((off_rows // 2, side), f32),
            vmem((n_y - 1, off_rows // 2, side), f32),
            vmem((2, off_rows, side), f32),
            vmem((n_hi - 1, out_rows, out_cols), f32),
            vmem((n_hi - 1, out_rows, out_cols), f32),
        ] + [dma(s) for s in sems],
        compiler_params=pltpu.CompilerParams(collective_id=0, has_side_effects=True),
    )(tiles, pair_list, pair_count, orbitals)
    return sums[0] + sums[1]


def solution(mesh):
    body = functools.partial(per_device, mesh.shape["aux"], mesh.shape["occ"])
    in_specs = (P("aux", "occ", None), P("aux", "occ", None), P("aux"), P())
    return jax.shard_map(body, mesh=mesh, in_specs=in_specs, out_specs=P("aux", "occ"), check_vma=False)
```

```python
import functools
import math

import jax
import jax.numpy as jnp
from jax import lax
from jax.experimental import pallas as pl
from jax.experimental.pallas import tpu as pltpu
from jax.sharding import PartitionSpec as P

LANES = 128
PIECES = 2
MESH = pl.DeviceIdType.MESH
NT = (((1,), (1,)), ((), ()))
NN = (((1,), (0,)), ((), ()))


def dot(a, b, dims):
    return lax.dot_general(a, b, dims, preferred_element_type=jnp.float32)


def split(x):
    hi = x.astype(jnp.bfloat16)
    return hi, (x - hi.astype(jnp.float32)).astype(jnp.bfloat16)


def kernel(n_aux, n_occ, n_sub, tiles, pairs_hbm, count_in, orb_hbm, out, pairs_in, orb, rx, rxd, ids, whi, wlo, hhi, hlo,
           dhi, dlo, diag, dcore, dfull, off, ocore, opair, oin, ofull, dense, z_in,
           in_s, local_s, tile_s, tile_r, quart_s, quart_r, ids_s, ids_r, idx_s, idx_r, dc_s, dc_r,
           dx_s, dx_r, dy_s, dy_r, df_s, df_r, dd_s, dd_r, oc_s, oc_r, oy_s, oy_r, ox_s, ox_r,
           op_s, op_r, of_s, of_r, z_s, z_r):
    a, o = lax.axis_index("aux"), lax.axis_index("occ")
    n_y, n_hi = n_occ // 2, n_aux // 2
    y, c = o // 2, lax.rem(o, 2)
    hi_a, lo = a // 2, lax.rem(a, 2)
    own_q = tiles.shape[0] // n_occ
    sub_q = own_q // n_sub
    krows = tiles.shape[1] // 2
    blk = 2 * krows
    side = 4 * blk
    n_slots = 2 * n_occ
    n_off = n_y * (n_y - 1) // 2
    d_half, o_half = side // 2, n_off * side // 2
    piece = o_half // PIECES
    nbf, n_orb = orb.shape[1], orb.shape[0]

    def y_peer(d):
        return lax.rem(y + d, n_y)

    peers = [(d, e) for d in range(1, n_y) for e in (0, 1)] + [(0, 1)]

    def occ_peer(d, e):
        return y_peer(d) * 2 + (c if e == 0 else 1 - c)

    partner = (a, occ_peer(0, 1))
    x_peer = (a + 1 - 2 * lo, o)

    def z_peer(d):
        return (lax.rem(hi_a + d, n_hi) * 2 + lo, o)

    barrier = pltpu.get_barrier_semaphore()
    greet = [(a, occ_peer(*d)) for d in peers] + [x_peer] + [z_peer(d) for d in range(1, n_hi)]
    for dev in greet:
        pl.semaphore_signal(barrier, inc=1, device_id=dev, device_id_type=MESH)

    def local(src, dst, s):
        cp = pltpu.make_async_copy(src, dst, s)
        cp.start()
        return cp

    def quarter(index):
        return tiles.at[pl.ds(index * own_q, own_q)]

    inputs = [local(src, dst, in_s.at[n]) for n, (src, dst) in enumerate(
        ((pairs_hbm, pairs_in), (orb_hbm, orb)))]
    locals_ = [local(quarter(o), rx.at[o], local_s.at[0])]
    for d in range(1, n_y):
        locals_.append(local(quarter(y_peer(d) * 2 + c), rxd.at[c, d - 1], local_s.at[d]))
    pl.semaphore_wait(barrier, len(greet))

    def remote(src, dst, s, r, dev):
        cp = pltpu.make_async_remote_copy(
            src_ref=src, dst_ref=dst, send_sem=s, recv_sem=r, device_id=dev, device_id_type=MESH
        )
        cp.start()
        return cp

    def sub_tiles(j, d, e):
        peer = occ_peer(d, e)
        n = d * 2 + e
        return remote(tiles.at[pl.ds(peer * own_q + j * sub_q, sub_q)], rx.at[o, pl.ds(j * sub_q, sub_q)],
                      tile_s.at[j, n], tile_r.at[j, n], (a, peer))

    def tiles_of(j):
        return [sub_tiles(j, d, e) for d in range(1, n_y) for e in (0, 1)]

    tile_copies = [tiles_of(0)]
    quarters = []
    inputs[0].wait()
    lane1 = lax.broadcasted_iota(jnp.int32, (8, LANES), 1)
    row1 = lax.broadcasted_iota(jnp.int32, (8, LANES), 0)
    within = lax.rem(lane1, blk)
    place = lax.rem(within, krows) * 2 + within // krows
    live = [jnp.where(o * 2 + s < count_in[0], pairs_in[0, s, 0] * blk, -nbf - blk) for s in range(2)]
    cols = jnp.where(row1 == 0, pairs_in[0, 0, 1], pairs_in[0, 1, 1]) * blk + within
    ids[lo, o] = jnp.where(row1 < 2, cols, jnp.where(lane1 < blk, live[0], live[1]) + place)
    id_copies = []
    for n, d in enumerate(peers):
        id_copies.append(remote(ids.at[lo, o], ids.at[lo, o], ids_s.at[n], ids_r.at[n], (a, occ_peer(*d))))
    for d in range(1, n_y):
        quarters.append(remote(quarter(y_peer(d) * 2 + 1 - c), rxd.at[c, d - 1],
                               quart_s.at[d], quart_r.at[d], partner))
    quarters.append(remote(quarter(o + 1 - 2 * c), rx.at[o], quart_s.at[0], quart_r.at[0], partner))
    for j in range(1, n_sub):
        tile_copies.append(tiles_of(j))
    inputs[1].wait()
    orb_hi, orb_lo = split(orb[...])
    row_pos = lax.broadcasted_iota(jnp.int32, (nbf, LANES), 0)
    lane = lax.broadcasted_iota(jnp.int32, (n_orb, LANES), 1)
    def weights(src):
        for s in range(2):
            sel = (row_pos == ids[lo, src, pl.ds(s, 1), :]).astype(jnp.float32).astype(jnp.bfloat16)
            for orb_part, copies, dst in ((orb_hi, 2, whi), (orb_lo, 1, wlo)):
                w = dot(orb_part, sel, NN)
                for p in range(2):
                    keep = lane < blk if p == 0 else lane >= blk
                    w_p = jnp.where(keep, w, 0.0).astype(jnp.bfloat16)
                    for n in range(copies):
                        dst[src * 2 + s, p * n_orb:(p + 1) * n_orb, n * LANES:(n + 1) * LANES] = w_p

    id_copies[-1].wait()
    for e in range(2):
        weights(y * 2 + e)

    def half(load, slot, row0, q0, hi_ref, lo_ref):
        rows = jnp.concatenate([load(q) for q in range(sub_q)], axis=0)
        bh, bl = split(rows)
        wh, wl = whi[slot], wlo[slot]
        res = dot(jnp.concatenate([bh, bl], axis=1), wh, NT) + dot(bh, wl, NT)
        for q in range(sub_q):
            for p in range(2):
                ph, pl_ = split(res[q * krows:(q + 1) * krows, p * n_orb:(p + 1) * n_orb])
                at = pl.ds(pl.multiple_of(row0 + p * krows, krows), krows)
                lanes = slice((q0 + q) * n_orb, (q0 + q + 1) * n_orb)
                hi_ref[at, lanes] = ph
                lo_ref[at, lanes] = pl_

    def gram(hi_i, lo_i, hi_k, lo_k):
        return dot(hi_i, hi_k, NT) + dot(hi_i, lo_k, NT) + dot(lo_i, hi_k, NT)

    for cp in locals_ + quarters:
        cp.wait()
    total = None
    for d in range(1, n_y):
        for j in range(n_sub):
            for e in range(2):
                for s in range(2):
                    half(lambda q: rxd[e, d - 1, j * sub_q + q, pl.ds(s, krows, stride=2), :],
                         (y * 2 + e) * 2 + s, (e * 2 + s) * blk, 0, dhi, dlo)
            val = gram(dhi[...], dlo[...], dhi[...], dlo[...])
            total = val if total is None else total + val
    mine = pl.ds(pl.multiple_of(y * side, side), side)
    for j in range(n_sub):
        for e in range(2):
            for s in range(2):
                half(lambda q: rx[y * 2 + e, j * sub_q + q, pl.ds(s, krows, stride=2), :],
                     (y * 2 + e) * 2 + s, ((y * 2 + e) * 2 + s) * blk, j * sub_q, hhi, hlo)
    total = total + gram(hhi[mine, :], hlo[mine, :], hhi[mine, :], hlo[mine, :])
    diag[...] = total
    cp = remote(diag.at[pl.ds((1 - c) * d_half, d_half)], dcore, dc_s, dc_r, partner)
    cp.wait()
    my_d = pl.ds(pl.multiple_of(c * d_half, d_half), d_half)
    dfull[lo, y, my_d, :] = diag[my_d, :] + dcore[...]
    my_diag = dfull.at[lo, y, my_d]
    dx = [remote(my_diag, my_diag, dx_s, dx_r, x_peer)]
    dys = [remote(my_diag, my_diag, dy_s.at[d], dy_r.at[d], (a, y_peer(d) * 2 + c)) for d in range(1, n_y)]

    for cp in id_copies[:-1]:
        cp.wait()
    idx_copy = remote(ids.at[lo], ids.at[lo], idx_s, idx_r, x_peer)
    for d in range(1, n_y):
        for e in range(2):
            weights(y_peer(d) * 2 + e)
    offs = [(i, k) for i in range(n_y) for k in range(i)]
    for j in range(n_sub):
        for cp in tile_copies[j]:
            cp.wait()
        for d in range(1, n_y):
            for e in range(2):
                for s in range(2):
                    src = y_peer(d) * 2 + e
                    half(lambda q: rx[src, j * sub_q + q, pl.ds(s, krows, stride=2), :],
                         src * 2 + s, (src * 2 + s) * blk, j * sub_q, hhi, hlo)
        at = slice(j * sub_q * n_orb, (j + 1) * sub_q * n_orb)
        for b, (i, k) in enumerate(offs):
            ri, rk = slice(i * side, (i + 1) * side), slice(k * side, (k + 1) * side)
            val = gram(hhi[ri, at], hlo[ri, at], hhi[rk, at], hlo[rk, at])
            if j:
                val = val + off[b * side:(b + 1) * side, :]
            off[b * side:(b + 1) * side, :] = val
    cp = remote(off.at[pl.ds((1 - c) * o_half, o_half)], ocore, oc_s, oc_r, partner)
    cp.wait()
    opair[...] = off[pl.ds(pl.multiple_of(c * o_half, piece), o_half), :] + ocore[...]
    oys = []
    for p in range(PIECES):
        at = pl.ds(p * piece, piece)
        oys.append([remote(opair.at[at], oin.at[d - 1, at], oy_s.at[p, d - 1], oy_r.at[p, d - 1],
                           (a, y_peer(d) * 2 + c)) for d in range(1, n_y)])
    dfs = []
    for d in range(1, n_y):
        dys[d - 1].wait_recv()
        got = dfull.at[lo, y_peer(n_y - d), my_d]
        dfs.append(remote(got, got, df_s.at[d], df_r.at[d], x_peer))
    oxs, ops = [], []
    for p in range(PIECES):
        val = opair[p * piece:(p + 1) * piece, :]
        for d in range(1, n_y):
            oys[p][d - 1].wait()
            val = val + oin[d - 1, p * piece:(p + 1) * piece, :]
        at = pl.ds(pl.multiple_of(c * o_half + p * piece, piece), piece)
        ofull[lo, at, :] = val
        ref = ofull.at[lo, at]
        oxs.append(remote(ref, ref, ox_s.at[p], ox_r.at[p], x_peer))
        ops.append(remote(ref, ref, op_s.at[p], op_r.at[p], partner))
    for cp in dx + dfs:
        cp.wait()
    for cp in dys:
        cp.wait_send()
    idx_copy.wait()
    half_d = dfull.at[:, :, my_d]
    cp = remote(half_d, half_d, dd_s, dd_r, partner)

    out_rows, out_cols = out.shape[1:]
    compact = n_slots * blk
    col_pos = lax.broadcasted_iota(jnp.int32, (out_cols, compact), 0) + o * out_cols
    row_i = lax.broadcasted_iota(jnp.int32, (n_hi * out_rows, compact), 0)
    row_h = lax.rem(row_i // out_rows + 1 + hi_a, n_hi)
    row_pos = (row_h * 2 + lo) * out_rows + lax.rem(row_i, out_rows)
    picks = []
    for l in range(2):
        where = jnp.concatenate([ids[l, s, 2:3, :] for s in range(n_occ)], axis=1)
        picks.append([(pos == where).astype(jnp.float32).astype(jnp.bfloat16) for pos in (col_pos, row_pos)])

    def spread(acc, l, i, t):
        for e in split(t):
            v = dot(picks[l][1][:, i * side:(i + 1) * side], e, NN)
            acc = v if acc is None else acc + v
        return acc

    cp.wait()
    acc = None
    for l in range(2):
        for i in range(n_y):
            dh, dl = split(dfull[l, i])
            cols = picks[l][0][:, i * side:(i + 1) * side]
            acc = spread(acc, l, i, dot(dh, cols, NT) + dot(dl, cols, NT))
    fwd = []
    for p in range(PIECES):
        oxs[p].wait()
        ref = ofull.at[1 - lo, pl.ds(pl.multiple_of(c * o_half + p * piece, piece), piece)]
        fwd.append(remote(ref, ref, of_s.at[p], of_r.at[p], partner))
    for cp in ops + fwd:
        cp.wait()
    parts = []
    for l in range(2):
        t = [None] * n_y
        for b, (i, k) in enumerate(offs):
            for e in split(ofull[l, b * side:(b + 1) * side, :]):
                vi = dot(e, picks[l][0][:, k * side:(k + 1) * side], NT)
                vk = dot(e, picks[l][0][:, i * side:(i + 1) * side], (((0,), (1,)), ((), ())))
                t[i] = vi if t[i] is None else t[i] + vi
                t[k] = vk if t[k] is None else t[k] + vk
        parts.append([split(v) for v in t])
    zs = []
    for g in range(n_hi // 2):
        rows = slice(2 * g * out_rows, 2 * (g + 1) * out_rows)
        v = acc[rows, :]
        for l in range(2):
            for i in range(n_y):
                for e in parts[l][i]:
                    v = v + dot(picks[l][1][rows, i * side:(i + 1) * side], e, NN)
        for n in range(2):
            d = 2 * g + n + 1
            if d < n_hi:
                dense[d - 1] = v[n * out_rows:(n + 1) * out_rows, :]
                zs.append(remote(dense.at[d - 1], z_in.at[d - 1], z_s.at[d - 1], z_r.at[d - 1], z_peer(d)))
            else:
                out[0] = v[n * out_rows:(n + 1) * out_rows, :]
    result = None
    for d in range(1, n_hi):
        zs[d - 1].wait()
        result = z_in[d - 1] if result is None else result + z_in[d - 1]
    out[1] = result


SHARES = (3, 2, 2, 1)
STREAM = len(SHARES)


def chunks(krows):
    unit, first = krows // sum(SHARES), 0
    spans = []
    for share in SHARES:
        spans.append((first * unit, share * unit))
        first += share
    return spans


def stream_kernel(n_hi, tiles, pairs_hbm, count_in, orb_hbm, out, pairs_in, orb, own, par, rx, ids, w_all, lhi, llo,
                  far, diag, off, p_l, p_f, acc, acc_in, in_s, own_s, par_s, par_r, y_s, y_r, ids_s, ids_r,
                  idz_s, idz_r, dz_s, dz_r, cz_s, cz_r, dd_s, dd_r, oz_s, oz_r, od_s, od_r, xy_s, xy_r, ready):
    a, o = lax.axis_index("aux"), lax.axis_index("occ")
    hi, lo, y, c = a // 2, lax.rem(a, 2), o // 2, lax.rem(o, 2)
    n_q, krows = tiles.shape[0], tiles.shape[1] // 2
    far_q, spans = n_q // 2, chunks(krows)
    blk, pair = 2 * krows, 4 * krows
    n_orb, nbf = orb.shape
    out_rows, out_cols = out.shape[1:]
    partner = (a, y * 2 + 1 - c)
    across = (a, (1 - y) * 2 + c)
    x_peer = (hi * 2 + 1 - lo, o)
    others = [(hi * 2 + 1 - lo, (1 - y) * 2 + c), x_peer, across]

    def z_peer(d):
        return (lax.rem(hi + d, n_hi) * 2 + lo, o)

    barrier = pltpu.get_barrier_semaphore()
    n_near = jnp.where(hi > 0, 1, 0) + jnp.where(hi < n_hi - 1, 1, 0)

    def greet(sem, devices):
        for dev in devices:
            pl.semaphore_signal(sem, inc=1, device_id=dev, device_id_type=MESH)

        @pl.when(hi > 0)
        def _():
            pl.semaphore_signal(sem, inc=1, device_id=(a - 2, o), device_id_type=MESH)

        @pl.when(hi < n_hi - 1)
        def _():
            pl.semaphore_signal(sem, inc=1, device_id=(a + 2, o), device_id_type=MESH)

    greet(barrier, [partner, across, x_peer])

    def local(src, dst, s):
        cp = pltpu.make_async_copy(src, dst, s)
        cp.start()
        return cp

    def remote(src, dst, s, r, dev):
        cp = pltpu.make_async_remote_copy(
            src_ref=src, dst_ref=dst, send_sem=s, recv_sem=r, device_id=dev, device_id_type=MESH
        )
        cp.start()
        return cp

    inputs = [local(src, dst, in_s.at[n]) for n, (src, dst) in enumerate(
        ((pairs_hbm, pairs_in), (orb_hbm, orb)))]
    halves = [pl.ds(n * far_q, far_q) for n in range(2)]
    own_copies = [local(tiles.at[h], own.at[h], own_s.at[n]) for n, h in enumerate(halves)]

    inputs[0].wait()
    lane1 = lax.broadcasted_iota(jnp.int32, (8, LANES), 1)
    row1 = lax.broadcasted_iota(jnp.int32, (8, LANES), 0)
    within = lax.rem(lane1, blk)
    place = lax.rem(within, krows) * 2 + within // krows
    live = [jnp.where(o * 2 + s < count_in[0], pairs_in[0, s, 0] * blk, -nbf - blk) for s in range(2)]
    cols = jnp.where(row1 == 0, pairs_in[0, 0, 1], pairs_in[0, 1, 1]) * blk + within
    near = jnp.where(lane1 < blk, live[0], live[1]) + place
    far_id = jnp.zeros((8, LANES), jnp.int32)
    for first, width in spans:
        at = lane1 - 4 * first
        tile_row = first * 2 + lax.rem(at, 2 * width)
        spot = jnp.where(lax.rem(tile_row, 2) == 0, live[0], live[1]) + tile_row // 2 * 2 + at // (2 * width)
        far_id = jnp.where((at >= 0) & (at < 4 * width), spot, far_id)
    ids[hi, o] = jnp.where(row1 < 2, cols, jnp.where(row1 == 2, near, far_id))

    pl.semaphore_wait(barrier, 3 + n_near)
    mine = ids.at[hi, o]

    id_copies = [remote(mine, mine, ids_s.at[n], ids_r.at[n], dev) for n, dev in enumerate((partner, across))]
    far_rows = pl.ds(pl.multiple_of((1 - y) * far_q, far_q), far_q)
    y_copies = [remote(tiles.at[far_rows, pl.ds(2 * first, 2 * width)], rx.at[:, pl.ds(2 * first, 2 * width)],
                       y_s.at[j], y_r.at[j], across) for j, (first, width) in enumerate(spans)]
    par_copies = [remote(tiles.at[h], par.at[h], par_s.at[n], par_r.at[n], partner) for n, h in enumerate(halves)]
    greet(ready.at[0], [partner, x_peer])
    inputs[1].wait()
    orb_hi, orb_lo = split(orb[...])
    row_pos = lax.broadcasted_iota(jnp.int32, (nbf, LANES), 0)
    lane = lax.broadcasted_iota(jnp.int32, (n_orb, LANES), 1)

    def weights(src, base):
        for s in range(2):
            sel = (row_pos == ids[hi, src, pl.ds(s, 1), :]).astype(jnp.float32).astype(jnp.bfloat16)
            for orb_part, spots in ((orb_hi, (0, 1)), (orb_lo, (2,))):
                w = dot(orb_part, sel, NN)
                for p in range(2):
                    keep = lane < blk if p == 0 else lane >= blk
                    w_p = jnp.where(keep, w, 0.0).astype(jnp.bfloat16)
                    for n in spots:
                        w_all[base + s, p * n_orb:(p + 1) * n_orb, n * LANES:(n + 1) * LANES] = w_p

    def transform(rows, slot):
        bh, bl = split(rows)
        return dot(jnp.concatenate([bh, bl, bh], axis=1), w_all[slot], NT)

    batch = math.gcd(far_q, 12)

    def near_half(src, e, base):
        def step(b, carry):
            for s in range(2):
                res = transform(jnp.concatenate(
                    [src[b * batch + q, pl.ds(s, krows, stride=2), :] for q in range(batch)], axis=0), base + s)
                for q in range(batch):
                    lanes = pl.ds(pl.multiple_of((b * batch + q) * n_orb, n_orb), n_orb)
                    for p in range(2):
                        h, l = split(res[q * krows:(q + 1) * krows, p * n_orb:(p + 1) * n_orb])
                        at = pl.ds(pl.multiple_of(e * pair + s * blk + p * krows, krows), krows)
                        lhi[at, lanes] = h
                        llo[at, lanes] = l
            return carry
        return step

    def stacked(both, hi_k):
        v = dot(both, hi_k, NT)
        n = v.shape[0] // 2
        return v[:n], v[n:]

    n_half = far_q // batch
    weights(o, 0)

    for n in range(2):
        own_copies[n].wait()
        lax.fori_loop(n * n_half, (n + 1) * n_half, near_half(own, c, 0), 0)
    pl.semaphore_wait(ready.at[0], 2 + n_near)
    if n_hi > 3:
        greet(ready.at[1], [])
    at = pl.ds(pl.multiple_of(c * pair, pair), pair)
    v, u = stacked(jnp.concatenate([lhi[at, :], llo[at, :]], axis=0), lhi[at, :])
    v = v + (u + u.T)
    diag[hi, c, 0:blk, :] = v[:blk]
    diag[hi, c, blk:pair - krows, :] = jnp.concatenate([v[blk:blk + krows, blk:], v[blk + krows:, blk:]], axis=1)
    for n in range(1, n_hi - 2):
        pl.semaphore_wait(ready.at[n], n_near)
        if n < n_hi - 3:
            greet(ready.at[n + 1], [])
    ref = diag.at[hi, c, pl.ds(0, pair - krows)]
    dz = [remote(ref, ref, dz_s.at[d - 1], dz_r.at[d - 1], z_peer(d)) for d in range(1, n_hi)]

    id_copies[0].wait()
    weights(y * 2 + 1 - c, 2)
    for n in range(2):
        par_copies[n].wait()
        lax.fori_loop(n * n_half, (n + 1) * n_half, near_half(par, 1 - c, 2), 0)
    at = pl.ds(pl.multiple_of(c * blk, blk), blk)
    right = slice(pair, 2 * pair)
    v, u = stacked(jnp.concatenate([lhi[at, :], llo[at, :]], axis=0), lhi[right, :])
    diag[hi, c, pair - krows:pair + krows, :] = v + u + dot(lhi[at, :], llo[right, :], NT)
    ref = diag.at[hi, c, pl.ds(pair - krows, blk)]
    dz += [remote(ref, ref, cz_s.at[d - 1], cz_r.at[d - 1], z_peer(d)) for d in range(1, n_hi)]

    id_copies[1].wait()
    theirs = ids.at[hi, (1 - y) * 2 + c]
    remote(theirs, theirs, ids_s.at[2], ids_r.at[2], partner).wait()
    ref = ids.at[hi]
    idz = [remote(ref, ref, idz_s.at[d - 1], idz_r.at[d - 1], z_peer(d)) for d in range(1, n_hi)]
    weights((1 - y) * 2 + c, 4)
    near_q = pl.ds(pl.multiple_of(y * far_q * n_orb, LANES), far_q * n_orb)

    def chunk_at(j):
        first, width = spans[j]
        return slice(4 * first, 4 * (first + width))

    def stream(j):
        first, width = spans[j]
        part, tall = 4 * width, 2 * width
        y_copies[j].wait()
        rows = jnp.concatenate([rx[q, 2 * first:2 * first + tall, :] for q in range(far_q)], axis=0)
        res = [transform(rows, 4 + s) for s in range(2)]
        even = lax.rem(lax.broadcasted_iota(jnp.int32, (tall, n_orb), 0), 2) == 0
        for q in range(far_q):
            at = slice(q * tall, (q + 1) * tall)
            both = [jnp.where(even, res[0][at, p * n_orb:(p + 1) * n_orb], res[1][at, p * n_orb:(p + 1) * n_orb])
                    for p in range(2)]
            h, l = split(jnp.concatenate(both, axis=0))
            far[0:part, q * n_orb:(q + 1) * n_orb] = h
            far[part:2 * part, q * n_orb:(q + 1) * n_orb] = l
        v = dot(lhi[:, near_q], far[0:2 * part, :], NT).T
        off[hi, c, chunk_at(j), :] = v[:part] + v[part:] + dot(llo[:, near_q], far[0:part, :], NT).T
        ref = off.at[hi, c, pl.ds(4 * first, part)]
        return [remote(ref, ref, oz_s.at[j, d - 1], oz_r.at[j, d - 1], z_peer(d)) for d in range(1, n_hi)]

    def share(copies, ref, s, r):
        for cp in copies:
            cp.wait()
        return remote(ref, ref, s, r, partner)

    def share_off(j):
        return share(oz[j], off.at[:, c, pl.ds(4 * spans[j][0], 4 * spans[j][1])], od_s.at[j], od_r.at[j])

    def onehot(pos, where):
        return (pos == where).astype(jnp.float32).astype(jnp.bfloat16)

    n_row = 2 * out_rows

    def positions(n):
        r = lax.broadcasted_iota(jnp.int32, (n_row, n), 0)
        r = jnp.where(r < out_rows, r + (1 - lo) * out_rows, r - (1 - lo) * out_rows) + hi * n_row
        col = lax.broadcasted_iota(jnp.int32, (out_cols, n), 0)
        return [r] + [col + (h * 2 + c) * out_cols for h in (1 - y, y)]

    def lanes_of(j):
        first, width = spans[j]
        return slice(n_hi * 8 * first, n_hi * 8 * (first + width))

    def place_ids():
        sides = [slice(0, n_row)] + [slice(n_row + h * out_cols, n_row + (h + 1) * out_cols) for h in range(2)]
        pos = positions(2 * pair)
        for g in range(n_hi):
            where = jnp.concatenate([ids[g, y * 2 + e, 2:3, :] for e in range(2)], axis=1)
            for span, at in zip(sides, pos):
                p_l[g, span, :] = onehot(at, where)
        for j in range(STREAM):
            where = jnp.concatenate([ids[g, (1 - y) * 2 + e, 3:4, chunk_at(j)]
                                     for g in range(n_hi) for e in range(2)], axis=1)
            for side, at in zip(sides, positions(where.shape[1])):
                p_f[side, lanes_of(j)] = onehot(at, where)

    def expand_diag():
        total = [None, None]
        for g in range(n_hi):
            rows = [p_l[g, 0:n_row, e * pair:(e + 1) * pair] for e in range(2)]
            cross = jnp.concatenate([diag[g, e, pair - krows:pair + krows, :] for e in range(2)], axis=0)
            t = [None, None]
            for e in range(2):
                top, low = diag[g, e, 0:blk, :], diag[g, e, blk:pair - krows, :]
                low = jnp.concatenate([low[:, :blk], low[:, blk:]], axis=0)
                both = jnp.concatenate([top, jnp.concatenate([top[:, blk:].T, low], axis=1)], axis=0)
                for v in split(both):
                    v = dot(rows[e], v, NN)
                    t[e] = v if t[e] is None else t[e] + v
            for v in split(cross):
                t[1] = t[1] + dot(rows[0], v, NN)
                t[0] = t[0] + dot(rows[1], v, NT)
            for v in split(jnp.concatenate(t, axis=1)):
                for h in range(2):
                    u = dot(v, p_l[g, n_row + h * out_cols:n_row + (h + 1) * out_cols, :], NT)
                    total[h] = u if total[h] is None else total[h] + u
        for h in range(2):
            for x in range(2):
                acc[x, h] = total[h][x * out_rows:(x + 1) * out_rows, :]

    def spread(j):
        rows, cols = [], [[], []]
        for g in range(n_hi):
            v = jnp.concatenate(split(jnp.concatenate([off[g, e, chunk_at(j), :] for e in range(2)], axis=0)), axis=0)
            v = dot(v, p_l[g], NT)
            n = v.shape[0] // 2
            v = v[:n] + v[n:]
            rows.append(v[:, 0:n_row])
            for h in range(2):
                cols[h].append(v[:, n_row + h * out_cols:n_row + (h + 1) * out_cols])
        rows = jnp.concatenate(rows, axis=0).T
        return (split(rows), [split(jnp.concatenate(v, axis=0)) for v in cols])

    def expand_off(j, after):
        rows, cols = spread(j)
        pick = p_f[0:n_row, lanes_of(j)]
        for h in range(2):
            v = dot(pick, cols[h][0], NN) + dot(pick, cols[h][1], NN)
            there = p_f[n_row + h * out_cols:n_row + (h + 1) * out_cols, lanes_of(j)]
            v = v + dot(rows[0], there, NT) + dot(rows[1], there, NT)
            for x in range(2):
                acc[x, h] += v[x * out_rows:(x + 1) * out_rows, :]
            after(h)

    def later(h):
        pass

    oz, od = [], []
    oz.append(stream(0))
    for cp in idz:
        cp.wait()
    place_ids()
    oz.append(stream(1))
    dd = share(dz, diag.at[:, c], dd_s, dd_r)
    oz.append(stream(2))
    od.append(share_off(0))
    dd.wait()
    expand_diag()
    oz.append(stream(3))
    od.append(share_off(1))
    od[0].wait()
    expand_off(0, later)
    od.append(share_off(2))
    for j in range(1, STREAM - 1):
        od[j].wait()
        expand_off(j, later)
    od.append(share_off(STREAM - 1))
    od[STREAM - 1].wait()
    sends = []

    def send(n, x, h):
        sends.append(remote(acc.at[x, h], acc_in.at[n], xy_s.at[n], xy_r.at[n], others[n]))

    def finish(h):
        send(h, 0, h)
        if h == 0:
            send(2, 1, 0)

    expand_off(STREAM - 1, finish)
    out[0] = acc[1, 1]
    for cp in sends:
        cp.wait()
    out[1] = acc_in[0] + acc_in[1] + acc_in[2]


def stream_call(n_hi, tiles, pair_list, pair_count, orbitals, out_rows, out_cols):
    n_q, rows2, _ = tiles.shape
    n_orb, _ = orbitals.shape
    krows = rows2 // 2
    far_q, blk, pair = n_q // 2, 2 * krows, 4 * krows
    part = max(4 * width for _, width in chunks(krows))
    n_pos = 2 * out_rows + 2 * out_cols
    f32, bf16, dma, vmem = jnp.float32, jnp.bfloat16, pltpu.SemaphoreType.DMA, pltpu.VMEM
    z = n_hi - 1
    sems = [(2,)] * 4 + [(STREAM,)] * 2 + [(3,)] * 2 + [(z,)] * 6 + [()] * 2 + [(STREAM, z)] * 2 + [(STREAM,)] * 2
    sems += [(3,)] * 2
    return pl.pallas_call(
        functools.partial(stream_kernel, n_hi),
        name="exchange",
        out_shape=jax.ShapeDtypeStruct((2, out_rows, out_cols), f32),
        in_specs=[pl.BlockSpec(memory_space=space) for space in (pl.ANY, pl.ANY, pltpu.SMEM, pl.ANY)],
        out_specs=pl.BlockSpec(memory_space=vmem),
        scratch_shapes=[
            pltpu.SMEM(pair_list.shape, jnp.int32),
            vmem(orbitals.shape, f32),
            vmem(tiles.shape, f32),
            vmem(tiles.shape, f32),
            vmem((far_q, 2 * krows, LANES), f32),
            vmem((n_hi, 4, 8, LANES), jnp.int32),
            vmem((6, 2 * n_orb, 3 * LANES), bf16),
            vmem((2 * pair, n_q * n_orb), bf16),
            vmem((2 * pair, n_q * n_orb), bf16),
            vmem((2 * part, far_q * n_orb), bf16),
            vmem((n_hi, 2, pair + krows, LANES), f32),
            vmem((n_hi, 2, pair, 2 * pair), f32),
            vmem((n_hi, n_pos, 2 * pair), bf16),
            vmem((n_pos, n_hi * 2 * pair), bf16),
            vmem((2, 2, out_rows, out_cols), f32),
            vmem((3, out_rows, out_cols), f32),
        ] + [dma(s) for s in sems] + [pltpu.SemaphoreType.REGULAR((max(n_hi - 2, 1),))],
        compiler_params=pltpu.CompilerParams(collective_id=0, has_side_effects=True),
    )(tiles, pair_list, pair_count, orbitals)


def per_device(n_aux, n_occ, blocks, pair_list, pair_count, orbitals):
    n_q, slots, area = blocks.shape
    n_orb, nbf = orbitals.shape
    krows = area // LANES
    blk = 2 * krows
    tiles = blocks.reshape(n_q, slots, krows, LANES).transpose(0, 2, 1, 3).reshape(n_q, krows * slots, LANES)
    if n_occ == 4 and slots * blk == LANES:
        sums = stream_call(n_aux // 2, tiles, pair_list, pair_count, orbitals, nbf // n_aux, nbf // n_occ)
        return sums[0] + sums[1]
    own_q = n_q // n_occ
    n_sub = math.gcd(own_q, 6)
    sub_k = own_q // n_sub * n_orb
    compact = slots * n_occ * blk
    side = 2 * slots * blk
    n_y, n_hi = n_occ // 2, n_aux // 2
    off_rows = n_y * (n_y - 1) // 2 * side
    out_rows, out_cols = nbf // n_aux, nbf // n_occ
    f32, bf16, dma, vmem = jnp.float32, jnp.bfloat16, pltpu.SemaphoreType.DMA, pltpu.VMEM
    sems = [(2,), (n_y,)] + [(n_sub, n_occ)] * 2 + [(n_y,)] * 2 + [(n_occ - 1,)] * 2 + [()] * 6 + [(n_y,)] * 4
    sems += [()] * 4 + [(PIECES, n_y - 1)] * 2 + [(PIECES,)] * 6 + [(n_hi - 1,)] * 2
    sums = pl.pallas_call(
        functools.partial(kernel, n_aux, n_occ, n_sub),
        name="exchange",
        out_shape=jax.ShapeDtypeStruct((2, out_rows, out_cols), f32),
        in_specs=[pl.BlockSpec(memory_space=space) for space in (pl.ANY, pl.ANY, pltpu.SMEM, pl.ANY)],
        out_specs=pl.BlockSpec(memory_space=vmem),
        scratch_shapes=[
            pltpu.SMEM(pair_list.shape, jnp.int32),
            vmem(orbitals.shape, f32),
            vmem((n_occ, own_q, krows * slots, LANES), f32),
            vmem((2, n_y - 1, own_q, krows * slots, LANES), f32),
            vmem((2, n_occ, 8, LANES), jnp.int32),
            vmem((slots * n_occ, 2 * n_orb, 2 * LANES), bf16),
            vmem((slots * n_occ, 2 * n_orb, LANES), bf16),
            vmem((compact, own_q * n_orb), bf16),
            vmem((compact, own_q * n_orb), bf16),
            vmem((side, sub_k), bf16),
            vmem((side, sub_k), bf16),
            vmem((side, side), f32),
            vmem((side // 2, side), f32),
            vmem((2, n_y, side, side), f32),
            vmem((off_rows, side), f32),
            vmem((off_rows // 2, side), f32),
            vmem((off_rows // 2, side), f32),
            vmem((n_y - 1, off_rows // 2, side), f32),
            vmem((2, off_rows, side), f32),
            vmem((n_hi - 1, out_rows, out_cols), f32),
            vmem((n_hi - 1, out_rows, out_cols), f32),
        ] + [dma(s) for s in sems],
        compiler_params=pltpu.CompilerParams(collective_id=0, has_side_effects=True),
    )(tiles, pair_list, pair_count, orbitals)
    return sums[0] + sums[1]


def solution(mesh):
    body = functools.partial(per_device, mesh.shape["aux"], mesh.shape["occ"])
    in_specs = (P("aux", "occ", None), P("aux", "occ", None), P("aux"), P())
    return jax.shard_map(body, mesh=mesh, in_specs=in_specs, out_specs=P("aux", "occ"), check_vma=False)
```

```python
import functools
import math

import jax
import jax.numpy as jnp
from jax import lax
from jax.experimental import pallas as pl
from jax.experimental.pallas import tpu as pltpu
from jax.sharding import PartitionSpec as P

LANES = 128
PIECES = 2
MESH = pl.DeviceIdType.MESH
NT = (((1,), (1,)), ((), ()))
NN = (((1,), (0,)), ((), ()))


def dot(a, b, dims):
    return lax.dot_general(a, b, dims, preferred_element_type=jnp.float32)


def split(x):
    hi = x.astype(jnp.bfloat16)
    return hi, (x - hi.astype(jnp.float32)).astype(jnp.bfloat16)


def kernel(n_aux, n_occ, n_sub, tiles, pairs_hbm, count_in, orb_hbm, out, pairs_in, orb, rx, rxd, ids, whi, wlo, hhi, hlo,
           dhi, dlo, diag, dcore, dfull, off, ocore, opair, oin, ofull, dense, z_in,
           in_s, local_s, tile_s, tile_r, quart_s, quart_r, ids_s, ids_r, idx_s, idx_r, dc_s, dc_r,
           dx_s, dx_r, dy_s, dy_r, df_s, df_r, dd_s, dd_r, oc_s, oc_r, oy_s, oy_r, ox_s, ox_r,
           op_s, op_r, of_s, of_r, z_s, z_r):
    a, o = lax.axis_index("aux"), lax.axis_index("occ")
    n_y, n_hi = n_occ // 2, n_aux // 2
    y, c = o // 2, lax.rem(o, 2)
    hi_a, lo = a // 2, lax.rem(a, 2)
    own_q = tiles.shape[0] // n_occ
    sub_q = own_q // n_sub
    krows = tiles.shape[1] // 2
    blk = 2 * krows
    side = 4 * blk
    n_slots = 2 * n_occ
    n_off = n_y * (n_y - 1) // 2
    d_half, o_half = side // 2, n_off * side // 2
    piece = o_half // PIECES
    nbf, n_orb = orb.shape[1], orb.shape[0]

    def y_peer(d):
        return lax.rem(y + d, n_y)

    peers = [(d, e) for d in range(1, n_y) for e in (0, 1)] + [(0, 1)]

    def occ_peer(d, e):
        return y_peer(d) * 2 + (c if e == 0 else 1 - c)

    partner = (a, occ_peer(0, 1))
    x_peer = (a + 1 - 2 * lo, o)

    def z_peer(d):
        return (lax.rem(hi_a + d, n_hi) * 2 + lo, o)

    barrier = pltpu.get_barrier_semaphore()
    greet = [(a, occ_peer(*d)) for d in peers] + [x_peer] + [z_peer(d) for d in range(1, n_hi)]
    for dev in greet:
        pl.semaphore_signal(barrier, inc=1, device_id=dev, device_id_type=MESH)

    def local(src, dst, s):
        cp = pltpu.make_async_copy(src, dst, s)
        cp.start()
        return cp

    def quarter(index):
        return tiles.at[pl.ds(index * own_q, own_q)]

    inputs = [local(src, dst, in_s.at[n]) for n, (src, dst) in enumerate(
        ((pairs_hbm, pairs_in), (orb_hbm, orb)))]
    locals_ = [local(quarter(o), rx.at[o], local_s.at[0])]
    for d in range(1, n_y):
        locals_.append(local(quarter(y_peer(d) * 2 + c), rxd.at[c, d - 1], local_s.at[d]))
    pl.semaphore_wait(barrier, len(greet))

    def remote(src, dst, s, r, dev):
        cp = pltpu.make_async_remote_copy(
            src_ref=src, dst_ref=dst, send_sem=s, recv_sem=r, device_id=dev, device_id_type=MESH
        )
        cp.start()
        return cp

    def sub_tiles(j, d, e):
        peer = occ_peer(d, e)
        n = d * 2 + e
        return remote(tiles.at[pl.ds(peer * own_q + j * sub_q, sub_q)], rx.at[o, pl.ds(j * sub_q, sub_q)],
                      tile_s.at[j, n], tile_r.at[j, n], (a, peer))

    def tiles_of(j):
        return [sub_tiles(j, d, e) for d in range(1, n_y) for e in (0, 1)]

    tile_copies = [tiles_of(0)]
    quarters = []
    inputs[0].wait()
    lane1 = lax.broadcasted_iota(jnp.int32, (8, LANES), 1)
    row1 = lax.broadcasted_iota(jnp.int32, (8, LANES), 0)
    within = lax.rem(lane1, blk)
    place = lax.rem(within, krows) * 2 + within // krows
    live = [jnp.where(o * 2 + s < count_in[0], pairs_in[0, s, 0] * blk, -nbf - blk) for s in range(2)]
    cols = jnp.where(row1 == 0, pairs_in[0, 0, 1], pairs_in[0, 1, 1]) * blk + within
    ids[lo, o] = jnp.where(row1 < 2, cols, jnp.where(lane1 < blk, live[0], live[1]) + place)
    id_copies = []
    for n, d in enumerate(peers):
        id_copies.append(remote(ids.at[lo, o], ids.at[lo, o], ids_s.at[n], ids_r.at[n], (a, occ_peer(*d))))
    for d in range(1, n_y):
        quarters.append(remote(quarter(y_peer(d) * 2 + 1 - c), rxd.at[c, d - 1],
                               quart_s.at[d], quart_r.at[d], partner))
    quarters.append(remote(quarter(o + 1 - 2 * c), rx.at[o], quart_s.at[0], quart_r.at[0], partner))
    for j in range(1, n_sub):
        tile_copies.append(tiles_of(j))
    inputs[1].wait()
    orb_hi, orb_lo = split(orb[...])
    row_pos = lax.broadcasted_iota(jnp.int32, (nbf, LANES), 0)
    lane = lax.broadcasted_iota(jnp.int32, (n_orb, LANES), 1)
    def weights(src):
        for s in range(2):
            sel = (row_pos == ids[lo, src, pl.ds(s, 1), :]).astype(jnp.float32).astype(jnp.bfloat16)
            for orb_part, copies, dst in ((orb_hi, 2, whi), (orb_lo, 1, wlo)):
                w = dot(orb_part, sel, NN)
                for p in range(2):
                    keep = lane < blk if p == 0 else lane >= blk
                    w_p = jnp.where(keep, w, 0.0).astype(jnp.bfloat16)
                    for n in range(copies):
                        dst[src * 2 + s, p * n_orb:(p + 1) * n_orb, n * LANES:(n + 1) * LANES] = w_p

    id_copies[-1].wait()
    for e in range(2):
        weights(y * 2 + e)

    def half(load, slot, row0, q0, hi_ref, lo_ref):
        rows = jnp.concatenate([load(q) for q in range(sub_q)], axis=0)
        bh, bl = split(rows)
        wh, wl = whi[slot], wlo[slot]
        res = dot(jnp.concatenate([bh, bl], axis=1), wh, NT) + dot(bh, wl, NT)
        for q in range(sub_q):
            for p in range(2):
                ph, pl_ = split(res[q * krows:(q + 1) * krows, p * n_orb:(p + 1) * n_orb])
                at = pl.ds(pl.multiple_of(row0 + p * krows, krows), krows)
                lanes = slice((q0 + q) * n_orb, (q0 + q + 1) * n_orb)
                hi_ref[at, lanes] = ph
                lo_ref[at, lanes] = pl_

    def gram(hi_i, lo_i, hi_k, lo_k):
        return dot(hi_i, hi_k, NT) + dot(hi_i, lo_k, NT) + dot(lo_i, hi_k, NT)

    for cp in locals_ + quarters:
        cp.wait()
    total = None
    for d in range(1, n_y):
        for j in range(n_sub):
            for e in range(2):
                for s in range(2):
                    half(lambda q: rxd[e, d - 1, j * sub_q + q, pl.ds(s, krows, stride=2), :],
                         (y * 2 + e) * 2 + s, (e * 2 + s) * blk, 0, dhi, dlo)
            val = gram(dhi[...], dlo[...], dhi[...], dlo[...])
            total = val if total is None else total + val
    mine = pl.ds(pl.multiple_of(y * side, side), side)
    for j in range(n_sub):
        for e in range(2):
            for s in range(2):
                half(lambda q: rx[y * 2 + e, j * sub_q + q, pl.ds(s, krows, stride=2), :],
                     (y * 2 + e) * 2 + s, ((y * 2 + e) * 2 + s) * blk, j * sub_q, hhi, hlo)
    total = total + gram(hhi[mine, :], hlo[mine, :], hhi[mine, :], hlo[mine, :])
    diag[...] = total
    cp = remote(diag.at[pl.ds((1 - c) * d_half, d_half)], dcore, dc_s, dc_r, partner)
    cp.wait()
    my_d = pl.ds(pl.multiple_of(c * d_half, d_half), d_half)
    dfull[lo, y, my_d, :] = diag[my_d, :] + dcore[...]
    my_diag = dfull.at[lo, y, my_d]
    dx = [remote(my_diag, my_diag, dx_s, dx_r, x_peer)]
    dys = [remote(my_diag, my_diag, dy_s.at[d], dy_r.at[d], (a, y_peer(d) * 2 + c)) for d in range(1, n_y)]

    for cp in id_copies[:-1]:
        cp.wait()
    idx_copy = remote(ids.at[lo], ids.at[lo], idx_s, idx_r, x_peer)
    for d in range(1, n_y):
        for e in range(2):
            weights(y_peer(d) * 2 + e)
    offs = [(i, k) for i in range(n_y) for k in range(i)]
    for j in range(n_sub):
        for cp in tile_copies[j]:
            cp.wait()
        for d in range(1, n_y):
            for e in range(2):
                for s in range(2):
                    src = y_peer(d) * 2 + e
                    half(lambda q: rx[src, j * sub_q + q, pl.ds(s, krows, stride=2), :],
                         src * 2 + s, (src * 2 + s) * blk, j * sub_q, hhi, hlo)
        at = slice(j * sub_q * n_orb, (j + 1) * sub_q * n_orb)
        for b, (i, k) in enumerate(offs):
            ri, rk = slice(i * side, (i + 1) * side), slice(k * side, (k + 1) * side)
            val = gram(hhi[ri, at], hlo[ri, at], hhi[rk, at], hlo[rk, at])
            if j:
                val = val + off[b * side:(b + 1) * side, :]
            off[b * side:(b + 1) * side, :] = val
    cp = remote(off.at[pl.ds((1 - c) * o_half, o_half)], ocore, oc_s, oc_r, partner)
    cp.wait()
    opair[...] = off[pl.ds(pl.multiple_of(c * o_half, piece), o_half), :] + ocore[...]
    oys = []
    for p in range(PIECES):
        at = pl.ds(p * piece, piece)
        oys.append([remote(opair.at[at], oin.at[d - 1, at], oy_s.at[p, d - 1], oy_r.at[p, d - 1],
                           (a, y_peer(d) * 2 + c)) for d in range(1, n_y)])
    dfs = []
    for d in range(1, n_y):
        dys[d - 1].wait_recv()
        got = dfull.at[lo, y_peer(n_y - d), my_d]
        dfs.append(remote(got, got, df_s.at[d], df_r.at[d], x_peer))
    oxs, ops = [], []
    for p in range(PIECES):
        val = opair[p * piece:(p + 1) * piece, :]
        for d in range(1, n_y):
            oys[p][d - 1].wait()
            val = val + oin[d - 1, p * piece:(p + 1) * piece, :]
        at = pl.ds(pl.multiple_of(c * o_half + p * piece, piece), piece)
        ofull[lo, at, :] = val
        ref = ofull.at[lo, at]
        oxs.append(remote(ref, ref, ox_s.at[p], ox_r.at[p], x_peer))
        ops.append(remote(ref, ref, op_s.at[p], op_r.at[p], partner))
    for cp in dx + dfs:
        cp.wait()
    for cp in dys:
        cp.wait_send()
    idx_copy.wait()
    half_d = dfull.at[:, :, my_d]
    cp = remote(half_d, half_d, dd_s, dd_r, partner)

    out_rows, out_cols = out.shape[1:]
    compact = n_slots * blk
    col_pos = lax.broadcasted_iota(jnp.int32, (out_cols, compact), 0) + o * out_cols
    row_i = lax.broadcasted_iota(jnp.int32, (n_hi * out_rows, compact), 0)
    row_h = lax.rem(row_i // out_rows + 1 + hi_a, n_hi)
    row_pos = (row_h * 2 + lo) * out_rows + lax.rem(row_i, out_rows)
    picks = []
    for l in range(2):
        where = jnp.concatenate([ids[l, s, 2:3, :] for s in range(n_occ)], axis=1)
        picks.append([(pos == where).astype(jnp.float32).astype(jnp.bfloat16) for pos in (col_pos, row_pos)])

    def spread(acc, l, i, t):
        for e in split(t):
            v = dot(picks[l][1][:, i * side:(i + 1) * side], e, NN)
            acc = v if acc is None else acc + v
        return acc

    cp.wait()
    acc = None
    for l in range(2):
        for i in range(n_y):
            dh, dl = split(dfull[l, i])
            cols = picks[l][0][:, i * side:(i + 1) * side]
            acc = spread(acc, l, i, dot(dh, cols, NT) + dot(dl, cols, NT))
    fwd = []
    for p in range(PIECES):
        oxs[p].wait()
        ref = ofull.at[1 - lo, pl.ds(pl.multiple_of(c * o_half + p * piece, piece), piece)]
        fwd.append(remote(ref, ref, of_s.at[p], of_r.at[p], partner))
    for cp in ops + fwd:
        cp.wait()
    parts = []
    for l in range(2):
        t = [None] * n_y
        for b, (i, k) in enumerate(offs):
            for e in split(ofull[l, b * side:(b + 1) * side, :]):
                vi = dot(e, picks[l][0][:, k * side:(k + 1) * side], NT)
                vk = dot(e, picks[l][0][:, i * side:(i + 1) * side], (((0,), (1,)), ((), ())))
                t[i] = vi if t[i] is None else t[i] + vi
                t[k] = vk if t[k] is None else t[k] + vk
        parts.append([split(v) for v in t])
    zs = []
    for g in range(n_hi // 2):
        rows = slice(2 * g * out_rows, 2 * (g + 1) * out_rows)
        v = acc[rows, :]
        for l in range(2):
            for i in range(n_y):
                for e in parts[l][i]:
                    v = v + dot(picks[l][1][rows, i * side:(i + 1) * side], e, NN)
        for n in range(2):
            d = 2 * g + n + 1
            if d < n_hi:
                dense[d - 1] = v[n * out_rows:(n + 1) * out_rows, :]
                zs.append(remote(dense.at[d - 1], z_in.at[d - 1], z_s.at[d - 1], z_r.at[d - 1], z_peer(d)))
            else:
                out[0] = v[n * out_rows:(n + 1) * out_rows, :]
    result = None
    for d in range(1, n_hi):
        zs[d - 1].wait()
        result = z_in[d - 1] if result is None else result + z_in[d - 1]
    out[1] = result


SHARES = (3, 2, 2, 1)
STREAM = len(SHARES)


def chunks(krows):
    unit, first = krows // sum(SHARES), 0
    spans = []
    for share in SHARES:
        spans.append((first * unit, share * unit))
        first += share
    return spans


def stream_kernel(n_hi, tiles, pairs_hbm, count_in, orb_hbm, out, pairs_in, orb, own, par, rx, ids, w_all, lhi, llo,
                  far, diag, off, p_l, p_f, acc, acc_in, in_s, own_s, par_s, par_r, y_s, y_r, ids_s, ids_r,
                  idz_s, idz_r, dz_s, dz_r, cz_s, cz_r, dd_s, dd_r, oz_s, oz_r, od_s, od_r, xy_s, xy_r, ready):
    a, o = lax.axis_index("aux"), lax.axis_index("occ")
    hi, lo, y, c = a // 2, lax.rem(a, 2), o // 2, lax.rem(o, 2)
    n_q, krows = tiles.shape[0], tiles.shape[1] // 2
    far_q, spans = n_q // 2, chunks(krows)
    blk, pair = 2 * krows, 4 * krows
    n_orb, nbf = orb.shape
    out_rows, out_cols = out.shape
    partner = (a, y * 2 + 1 - c)
    across = (a, (1 - y) * 2 + c)
    x_peer = (hi * 2 + 1 - lo, o)
    others = [(hi * 2 + 1 - lo, (1 - y) * 2 + c), x_peer, across]

    def z_peer(d):
        return (lax.rem(hi + d, n_hi) * 2 + lo, o)

    barrier = pltpu.get_barrier_semaphore()
    n_near = jnp.where(hi > 0, 1, 0) + jnp.where(hi < n_hi - 1, 1, 0)

    def greet(sem, devices):
        for dev in devices:
            pl.semaphore_signal(sem, inc=1, device_id=dev, device_id_type=MESH)

        @pl.when(hi > 0)
        def _():
            pl.semaphore_signal(sem, inc=1, device_id=(a - 2, o), device_id_type=MESH)

        @pl.when(hi < n_hi - 1)
        def _():
            pl.semaphore_signal(sem, inc=1, device_id=(a + 2, o), device_id_type=MESH)

    greet(barrier, [partner, across, x_peer])

    def local(src, dst, s):
        cp = pltpu.make_async_copy(src, dst, s)
        cp.start()
        return cp

    def remote(src, dst, s, r, dev):
        cp = pltpu.make_async_remote_copy(
            src_ref=src, dst_ref=dst, send_sem=s, recv_sem=r, device_id=dev, device_id_type=MESH
        )
        cp.start()
        return cp

    inputs = [local(src, dst, in_s.at[n]) for n, (src, dst) in enumerate(
        ((pairs_hbm, pairs_in), (orb_hbm, orb)))]
    halves = [pl.ds(n * far_q, far_q) for n in range(2)]
    own_copies = [local(tiles.at[h], own.at[h], own_s.at[n]) for n, h in enumerate(halves)]

    inputs[0].wait()
    lane1 = lax.broadcasted_iota(jnp.int32, (8, LANES), 1)
    row1 = lax.broadcasted_iota(jnp.int32, (8, LANES), 0)
    within = lax.rem(lane1, blk)
    place = lax.rem(within, krows) * 2 + within // krows
    live = [jnp.where(o * 2 + s < count_in[0], pairs_in[0, s, 0] * blk, -nbf - blk) for s in range(2)]
    cols = jnp.where(row1 == 0, pairs_in[0, 0, 1], pairs_in[0, 1, 1]) * blk + within
    near = jnp.where(lane1 < blk, live[0], live[1]) + place
    far_id = jnp.zeros((8, LANES), jnp.int32)
    for first, width in spans:
        at = lane1 - 4 * first
        tile_row = first * 2 + lax.rem(at, 2 * width)
        spot = jnp.where(lax.rem(tile_row, 2) == 0, live[0], live[1]) + tile_row // 2 * 2 + at // (2 * width)
        far_id = jnp.where((at >= 0) & (at < 4 * width), spot, far_id)
    ids[hi, o] = jnp.where(row1 < 2, cols, jnp.where(row1 == 2, near, far_id))

    pl.semaphore_wait(barrier, 3 + n_near)
    mine = ids.at[hi, o]

    id_copies = [remote(mine, mine, ids_s.at[n], ids_r.at[n], dev) for n, dev in enumerate((partner, across))]
    far_rows = pl.ds(pl.multiple_of((1 - y) * far_q, far_q), far_q)
    y_copies = [remote(tiles.at[far_rows, pl.ds(2 * first, 2 * width)], rx.at[:, pl.ds(2 * first, 2 * width)],
                       y_s.at[j], y_r.at[j], across) for j, (first, width) in enumerate(spans)]
    par_copies = [remote(tiles.at[h], par.at[h], par_s.at[n], par_r.at[n], partner) for n, h in enumerate(halves)]
    greet(ready.at[0], [partner, x_peer])
    inputs[1].wait()
    orb_hi, orb_lo = split(orb[...])
    row_pos = lax.broadcasted_iota(jnp.int32, (nbf, LANES), 0)
    lane = lax.broadcasted_iota(jnp.int32, (n_orb, LANES), 1)

    def weights(src, base):
        for s in range(2):
            sel = (row_pos == ids[hi, src, pl.ds(s, 1), :]).astype(jnp.float32).astype(jnp.bfloat16)
            for orb_part, spots in ((orb_hi, (0, 1)), (orb_lo, (2,))):
                w = dot(orb_part, sel, NN)
                for p in range(2):
                    keep = lane < blk if p == 0 else lane >= blk
                    w_p = jnp.where(keep, w, 0.0).astype(jnp.bfloat16)
                    for n in spots:
                        w_all[base + s, p * n_orb:(p + 1) * n_orb, n * LANES:(n + 1) * LANES] = w_p

    def transform(rows, slot):
        bh, bl = split(rows)
        return dot(jnp.concatenate([bh, bl, bh], axis=1), w_all[slot], NT)

    batch = math.gcd(far_q, 12)

    def near_half(src, e, base):
        def step(b, carry):
            for s in range(2):
                res = transform(jnp.concatenate(
                    [src[b * batch + q, pl.ds(s, krows, stride=2), :] for q in range(batch)], axis=0), base + s)
                for q in range(batch):
                    lanes = pl.ds(pl.multiple_of((b * batch + q) * n_orb, n_orb), n_orb)
                    for p in range(2):
                        h, l = split(res[q * krows:(q + 1) * krows, p * n_orb:(p + 1) * n_orb])
                        at = pl.ds(pl.multiple_of(e * pair + s * blk + p * krows, krows), krows)
                        lhi[at, lanes] = h
                        llo[at, lanes] = l
            return carry
        return step

    def stacked(both, hi_k):
        v = dot(both, hi_k, NT)
        n = v.shape[0] // 2
        return v[:n], v[n:]

    n_half = far_q // batch
    weights(o, 0)

    for n in range(2):
        own_copies[n].wait()
        lax.fori_loop(n * n_half, (n + 1) * n_half, near_half(own, c, 0), 0)
    pl.semaphore_wait(ready.at[0], 2 + n_near)
    if n_hi > 3:
        greet(ready.at[1], [])
    at = pl.ds(pl.multiple_of(c * pair, pair), pair)
    v, u = stacked(jnp.concatenate([lhi[at, :], llo[at, :]], axis=0), lhi[at, :])
    v = v + (u + u.T)
    diag[hi, c, 0:blk, :] = v[:blk]
    diag[hi, c, blk:pair - krows, :] = jnp.concatenate([v[blk:blk + krows, blk:], v[blk + krows:, blk:]], axis=1)
    for n in range(1, n_hi - 2):
        pl.semaphore_wait(ready.at[n], n_near)
        if n < n_hi - 3:
            greet(ready.at[n + 1], [])
    ref = diag.at[hi, c, pl.ds(0, pair - krows)]
    dz = [remote(ref, ref, dz_s.at[d - 1], dz_r.at[d - 1], z_peer(d)) for d in range(1, n_hi)]

    id_copies[0].wait()
    weights(y * 2 + 1 - c, 2)
    for n in range(2):
        par_copies[n].wait()
        lax.fori_loop(n * n_half, (n + 1) * n_half, near_half(par, 1 - c, 2), 0)
    at = pl.ds(pl.multiple_of(c * blk, blk), blk)
    right = slice(pair, 2 * pair)
    v, u = stacked(jnp.concatenate([lhi[at, :], llo[at, :]], axis=0), lhi[right, :])
    diag[hi, c, pair - krows:pair + krows, :] = v + u + dot(lhi[at, :], llo[right, :], NT)
    ref = diag.at[hi, c, pl.ds(pair - krows, blk)]
    dz += [remote(ref, ref, cz_s.at[d - 1], cz_r.at[d - 1], z_peer(d)) for d in range(1, n_hi)]

    id_copies[1].wait()
    theirs = ids.at[hi, (1 - y) * 2 + c]
    remote(theirs, theirs, ids_s.at[2], ids_r.at[2], partner).wait()
    ref = ids.at[hi]
    idz = [remote(ref, ref, idz_s.at[d - 1], idz_r.at[d - 1], z_peer(d)) for d in range(1, n_hi)]
    weights((1 - y) * 2 + c, 4)
    near_q = pl.ds(pl.multiple_of(y * far_q * n_orb, LANES), far_q * n_orb)

    def chunk_at(j):
        first, width = spans[j]
        return slice(4 * first, 4 * (first + width))

    def stream(j):
        first, width = spans[j]
        part, tall = 4 * width, 2 * width
        y_copies[j].wait()
        rows = jnp.concatenate([rx[q, 2 * first:2 * first + tall, :] for q in range(far_q)], axis=0)
        res = [transform(rows, 4 + s) for s in range(2)]
        even = lax.rem(lax.broadcasted_iota(jnp.int32, (tall, n_orb), 0), 2) == 0
        for q in range(far_q):
            at = slice(q * tall, (q + 1) * tall)
            both = [jnp.where(even, res[0][at, p * n_orb:(p + 1) * n_orb], res[1][at, p * n_orb:(p + 1) * n_orb])
                    for p in range(2)]
            h, l = split(jnp.concatenate(both, axis=0))
            far[0:part, q * n_orb:(q + 1) * n_orb] = h
            far[part:2 * part, q * n_orb:(q + 1) * n_orb] = l
        v = dot(lhi[:, near_q], far[0:2 * part, :], NT).T
        off[hi, c, chunk_at(j), :] = v[:part] + v[part:] + dot(llo[:, near_q], far[0:part, :], NT).T
        ref = off.at[hi, c, pl.ds(4 * first, part)]
        return [remote(ref, ref, oz_s.at[j, d - 1], oz_r.at[j, d - 1], z_peer(d)) for d in range(1, n_hi)]

    def share(copies, ref, s, r):
        for cp in copies:
            cp.wait()
        return remote(ref, ref, s, r, partner)

    def share_off(j):
        return share(oz[j], off.at[:, c, pl.ds(4 * spans[j][0], 4 * spans[j][1])], od_s.at[j], od_r.at[j])

    def onehot(pos, where):
        return (pos == where).astype(jnp.float32).astype(jnp.bfloat16)

    n_row = 2 * out_rows

    def positions(n):
        r = lax.broadcasted_iota(jnp.int32, (n_row, n), 0)
        r = jnp.where(r < out_rows, r + (1 - lo) * out_rows, r - (1 - lo) * out_rows) + hi * n_row
        col = lax.broadcasted_iota(jnp.int32, (out_cols, n), 0)
        return [r] + [col + (h * 2 + c) * out_cols for h in (1 - y, y)]

    def lanes_of(j):
        first, width = spans[j]
        return slice(n_hi * 8 * first, n_hi * 8 * (first + width))

    def place_ids():
        sides = [slice(0, n_row)] + [slice(n_row + h * out_cols, n_row + (h + 1) * out_cols) for h in range(2)]
        pos = positions(2 * pair)
        for g in range(n_hi):
            where = jnp.concatenate([ids[g, y * 2 + e, 2:3, :] for e in range(2)], axis=1)
            for span, at in zip(sides, pos):
                p_l[g, span, :] = onehot(at, where)
        for j in range(STREAM):
            where = jnp.concatenate([ids[g, (1 - y) * 2 + e, 3:4, chunk_at(j)]
                                     for g in range(n_hi) for e in range(2)], axis=1)
            for side, at in zip(sides, positions(where.shape[1])):
                p_f[side, lanes_of(j)] = onehot(at, where)

    def expand_diag():
        total = [None, None]
        for g in range(n_hi):
            rows = [p_l[g, 0:n_row, e * pair:(e + 1) * pair] for e in range(2)]
            cross = jnp.concatenate([diag[g, e, pair - krows:pair + krows, :] for e in range(2)], axis=0)
            t = [None, None]
            for e in range(2):
                top, low = diag[g, e, 0:blk, :], diag[g, e, blk:pair - krows, :]
                low = jnp.concatenate([low[:, :blk], low[:, blk:]], axis=0)
                both = jnp.concatenate([top, jnp.concatenate([top[:, blk:].T, low], axis=1)], axis=0)
                for v in split(both):
                    v = dot(rows[e], v, NN)
                    t[e] = v if t[e] is None else t[e] + v
            for v in split(cross):
                t[1] = t[1] + dot(rows[0], v, NN)
                t[0] = t[0] + dot(rows[1], v, NT)
            for v in split(jnp.concatenate(t, axis=1)):
                for h in range(2):
                    u = dot(v, p_l[g, n_row + h * out_cols:n_row + (h + 1) * out_cols, :], NT)
                    total[h] = u if total[h] is None else total[h] + u
        for h in range(2):
            for x in range(2):
                acc[x, h] = total[h][x * out_rows:(x + 1) * out_rows, :]

    def spread(j):
        rows, cols = [], [[], []]
        for g in range(n_hi):
            v = jnp.concatenate(split(jnp.concatenate([off[g, e, chunk_at(j), :] for e in range(2)], axis=0)), axis=0)
            v = dot(v, p_l[g], NT)
            n = v.shape[0] // 2
            v = v[:n] + v[n:]
            rows.append(v[:, 0:n_row])
            for h in range(2):
                cols[h].append(v[:, n_row + h * out_cols:n_row + (h + 1) * out_cols])
        rows = jnp.concatenate(rows, axis=0).T
        return (split(rows), [split(jnp.concatenate(v, axis=0)) for v in cols])

    def expand_off(j, after):
        rows, cols = spread(j)
        pick = p_f[0:n_row, lanes_of(j)]
        for h in range(2):
            v = dot(pick, cols[h][0], NN) + dot(pick, cols[h][1], NN)
            there = p_f[n_row + h * out_cols:n_row + (h + 1) * out_cols, lanes_of(j)]
            v = v + dot(rows[0], there, NT) + dot(rows[1], there, NT)
            for x in range(2):
                acc[x, h] += v[x * out_rows:(x + 1) * out_rows, :]
            after(h)

    def later(h):
        pass

    oz, od = [], []
    oz.append(stream(0))
    for cp in idz:
        cp.wait()
    place_ids()
    oz.append(stream(1))
    dd = share(dz, diag.at[:, c], dd_s, dd_r)
    oz.append(stream(2))
    od.append(share_off(0))
    dd.wait()
    expand_diag()
    oz.append(stream(3))
    od.append(share_off(1))
    od[0].wait()
    expand_off(0, later)
    od.append(share_off(2))
    for j in range(1, STREAM - 1):
        od[j].wait()
        expand_off(j, later)
    od.append(share_off(STREAM - 1))
    od[STREAM - 1].wait()
    sends = []

    def send(n, x, h):
        sends.append(remote(acc.at[x, h], acc_in.at[n], xy_s.at[n], xy_r.at[n], others[n]))

    def finish(h):
        send(h, 0, h)
        if h == 0:
            send(2, 1, 0)

    expand_off(STREAM - 1, finish)
    for cp in sends:
        cp.wait()
    out[...] = acc[1, 1] + acc_in[0] + acc_in[1] + acc_in[2]


def stream_call(n_hi, tiles, pair_list, pair_count, orbitals, out_rows, out_cols):
    n_q, rows2, _ = tiles.shape
    n_orb, _ = orbitals.shape
    krows = rows2 // 2
    far_q, blk, pair = n_q // 2, 2 * krows, 4 * krows
    part = max(4 * width for _, width in chunks(krows))
    n_pos = 2 * out_rows + 2 * out_cols
    f32, bf16, dma, vmem = jnp.float32, jnp.bfloat16, pltpu.SemaphoreType.DMA, pltpu.VMEM
    z = n_hi - 1
    sems = [(2,)] * 4 + [(STREAM,)] * 2 + [(3,)] * 2 + [(z,)] * 6 + [()] * 2 + [(STREAM, z)] * 2 + [(STREAM,)] * 2
    sems += [(3,)] * 2
    return pl.pallas_call(
        functools.partial(stream_kernel, n_hi),
        name="exchange",
        out_shape=jax.ShapeDtypeStruct((out_rows, out_cols), f32),
        in_specs=[pl.BlockSpec(memory_space=space) for space in (pl.ANY, pl.ANY, pltpu.SMEM, pl.ANY)],
        out_specs=pl.BlockSpec(memory_space=vmem),
        scratch_shapes=[
            pltpu.SMEM(pair_list.shape, jnp.int32),
            vmem(orbitals.shape, f32),
            vmem(tiles.shape, f32),
            vmem(tiles.shape, f32),
            vmem((far_q, 2 * krows, LANES), f32),
            vmem((n_hi, 4, 8, LANES), jnp.int32),
            vmem((6, 2 * n_orb, 3 * LANES), bf16),
            vmem((2 * pair, n_q * n_orb), bf16),
            vmem((2 * pair, n_q * n_orb), bf16),
            vmem((2 * part, far_q * n_orb), bf16),
            vmem((n_hi, 2, pair + krows, LANES), f32),
            vmem((n_hi, 2, pair, 2 * pair), f32),
            vmem((n_hi, n_pos, 2 * pair), bf16),
            vmem((n_pos, n_hi * 2 * pair), bf16),
            vmem((2, 2, out_rows, out_cols), f32),
            vmem((3, out_rows, out_cols), f32),
        ] + [dma(s) for s in sems] + [pltpu.SemaphoreType.REGULAR((max(n_hi - 2, 1),))],
        compiler_params=pltpu.CompilerParams(collective_id=0, has_side_effects=True),
    )(tiles, pair_list, pair_count, orbitals)


def per_device(n_aux, n_occ, blocks, pair_list, pair_count, orbitals):
    n_q, slots, area = blocks.shape
    n_orb, nbf = orbitals.shape
    krows = area // LANES
    blk = 2 * krows
    tiles = blocks.reshape(n_q, slots, krows, LANES).transpose(0, 2, 1, 3).reshape(n_q, krows * slots, LANES)
    if n_occ == 4 and slots * blk == LANES:
        sums = stream_call(n_aux // 2, tiles, pair_list, pair_count, orbitals, nbf // n_aux, nbf // n_occ)
        return sums
    own_q = n_q // n_occ
    n_sub = math.gcd(own_q, 6)
    sub_k = own_q // n_sub * n_orb
    compact = slots * n_occ * blk
    side = 2 * slots * blk
    n_y, n_hi = n_occ // 2, n_aux // 2
    off_rows = n_y * (n_y - 1) // 2 * side
    out_rows, out_cols = nbf // n_aux, nbf // n_occ
    f32, bf16, dma, vmem = jnp.float32, jnp.bfloat16, pltpu.SemaphoreType.DMA, pltpu.VMEM
    sems = [(2,), (n_y,)] + [(n_sub, n_occ)] * 2 + [(n_y,)] * 2 + [(n_occ - 1,)] * 2 + [()] * 6 + [(n_y,)] * 4
    sems += [()] * 4 + [(PIECES, n_y - 1)] * 2 + [(PIECES,)] * 6 + [(n_hi - 1,)] * 2
    sums = pl.pallas_call(
        functools.partial(kernel, n_aux, n_occ, n_sub),
        name="exchange",
        out_shape=jax.ShapeDtypeStruct((2, out_rows, out_cols), f32),
        in_specs=[pl.BlockSpec(memory_space=space) for space in (pl.ANY, pl.ANY, pltpu.SMEM, pl.ANY)],
        out_specs=pl.BlockSpec(memory_space=vmem),
        scratch_shapes=[
            pltpu.SMEM(pair_list.shape, jnp.int32),
            vmem(orbitals.shape, f32),
            vmem((n_occ, own_q, krows * slots, LANES), f32),
            vmem((2, n_y - 1, own_q, krows * slots, LANES), f32),
            vmem((2, n_occ, 8, LANES), jnp.int32),
            vmem((slots * n_occ, 2 * n_orb, 2 * LANES), bf16),
            vmem((slots * n_occ, 2 * n_orb, LANES), bf16),
            vmem((compact, own_q * n_orb), bf16),
            vmem((compact, own_q * n_orb), bf16),
            vmem((side, sub_k), bf16),
            vmem((side, sub_k), bf16),
            vmem((side, side), f32),
            vmem((side // 2, side), f32),
            vmem((2, n_y, side, side), f32),
            vmem((off_rows, side), f32),
            vmem((off_rows // 2, side), f32),
            vmem((off_rows // 2, side), f32),
            vmem((n_y - 1, off_rows // 2, side), f32),
            vmem((2, off_rows, side), f32),
            vmem((n_hi - 1, out_rows, out_cols), f32),
            vmem((n_hi - 1, out_rows, out_cols), f32),
        ] + [dma(s) for s in sems],
        compiler_params=pltpu.CompilerParams(collective_id=0, has_side_effects=True),
    )(tiles, pair_list, pair_count, orbitals)
    return sums[0] + sums[1]


def solution(mesh):
    body = functools.partial(per_device, mesh.shape["aux"], mesh.shape["occ"])
    in_specs = (P("aux", "occ", None), P("aux", "occ", None), P("aux"), P())
    return jax.shard_map(body, mesh=mesh, in_specs=in_specs, out_specs=P("aux", "occ"), check_vma=False)
```
